512 devices in a mesh: ra: 64 (over z_lo, x, core), dec: 8 (over y, z_hi).
Axes of the slice: x: 4, y: 4, z: 16 (z_hi: 2, z_lo: 8; z = z_hi * 8 + z_lo), core: 2. Of those that a mesh axis runs over, the one named last changes fastest.
Arguments:
- exposure: float32 [131072, 2048], P(('ra', 'dec')), may hold values from -6 to 6
- slots: int32 [131072, 1], P(('ra', 'dec')), may hold values from 0 to 4; in each aligned block of 256 rows (0 to 255, 256 to 511, ...) at most 128 rows name the same one
- target_rows: int32 [131072], P(('ra', 'dec')), may hold values from 0 to 63
- template: bfloat16 [512, 131072], P('dec', 'ra'), may hold values from -6 to 6
- row_taps: bfloat16 [45, 21], replicated, may hold values from -1.25 to 1.25
- col_taps: bfloat16 [45, 21], replicated, may hold values from -1.25 to 1.25
- coef: float32 [45, 6], replicated, may hold values from -0.6 to 0.6
Outputs:
- difference: float32 [512, 131072], P('dec', 'ra')
The draws below stay inside these ranges and needn't reach their ends.
Inputs may be any that keep to these rules, and one draw needn't show every extreme that they name: `slots`: among the rows of one device no value is taken by more than 128 rows; on some devices some value is taken by exactly 128.
All inputs are finite; a program needn't handle non-finite values.
Results may differ from the reference program's by a relative error of at most 0.0017.
Values may be sent and summed in bfloat16 or wider, within the bound.
A program may use at most 64 MiB of HBM per device.

```python
import math
import jax
import jax.numpy as jnp
import numpy as np
from jax import lax

W = 2048
PR = 64
E_DEV = 256
K = 45
TAPS = 21
TERMS = 6
SPAN = 2
HALF = 10
CAP = 128
NROWS = 512
NCOLS = 131072
EXPROWS = 131072
N_RA = 64
N_DEC = 8


def plant(result, key, least, high):
    place = [jax.random.randint(jax.random.fold_in(key, axis), (), 0, length) for axis, length in enumerate(result.shape)]
    widest = result.shape.index(max(result.shape))
    next_to = place[:widest] + [(place[widest] + 1) % result.shape[widest]] + place[widest + 1:]
    return result.at[tuple(place)].set(least).at[tuple(next_to)].set(high)


def level_of(key, dims, pieces, low, largest):
    factor_of = 1.0
    for axis_at, blocks in pieces:
        steps = jax.random.uniform(jax.random.fold_in(jax.random.fold_in(key, 6), axis_at), (blocks,), jnp.float32, low / len(pieces), largest / len(pieces))
        factor_of = factor_of * jnp.repeat(jnp.exp(steps), dims[axis_at] // blocks).reshape((-1,) + (1,) * (len(dims) - 1 - axis_at))
    return factor_of


def assign_block(rng, own, number, rows, amount, top, bound, skew):
    order = jax.random.permutation(rng, amount)
    packed, usual = load_shares(amount, rows * top, bound, skew, True), load_shares(amount, rows * top, bound, skew, False)
    places = jnp.arange(amount)

    def named(lengths, rotation):
        used = int((lengths > 0).sum())
        fixed = max(1, used // 4)
        moved = fixed + (places - fixed + rotation * (used - fixed)) % max(1, amount - fixed)
        return jnp.zeros((amount,), jnp.int32).at[order[jnp.where(places < fixed, places, moved)]].set(jnp.asarray(lengths, jnp.int32))

    lengths = jnp.where(number % 4 == 0, named(packed, number // 4), named(usual, number - number // 4 - 1))
    mixed = jax.random.permutation(jax.random.fold_in(own, 3), amount)
    source_of, sink = mixed[0:amount // 2 * 2:2], mixed[1:amount // 2 * 2:2]
    room = jnp.minimum(lengths[source_of] - 1, bound - lengths[sink]) // 2
    room = jnp.where((source_of == order[0]) | (sink == order[0]) | (lengths[sink] == 0), 0, jnp.maximum(room, 0))
    moved = jax.random.randint(jax.random.fold_in(own, 4), (amount // 2,), 0, 1 << 20) % (room + 1)
    lengths = lengths.at[source_of].add(-moved).at[sink].add(moved)
    labels = jnp.searchsorted(jnp.cumsum(lengths), jnp.arange(rows * top), side="right").astype(jnp.int32)
    listing = labels.reshape(top, rows).T
    listing = listing[jax.random.permutation(jax.random.fold_in(own, 1), rows)]
    rotation = jax.random.randint(jax.random.fold_in(own, 2), (rows, 1), 0, top)
    return jnp.take_along_axis(listing, (jnp.arange(top)[None, :] + rotation) % top, axis=1)


def load_shares(number_of, total, reach, slope, full):
    portions = [(1 << 20) // math.isqrt(standing ** slope) + 1 for standing in range(1, number_of + 1)]
    largest = reach if full else min(reach, max(-(-total // number_of), total * portions[0] // sum(portions)))
    least = 1 if total - largest >= number_of - 1 else 0
    counts, surplus = [largest] + [least] * (number_of - 1), total - largest - least * (number_of - 1)
    while surplus > 0:
        free = [i for i in range(1, number_of) if counts[i] < largest] or [i for i in range(1, number_of) if counts[i] < reach]
        pool, left = sum([portions[i] for i in free]), surplus
        for i in free:
            addition = min(reach - counts[i], max(1, left * portions[i] // pool), surplus)
            counts[i] = counts[i] + addition
            surplus = surplus - addition
    return np.array(counts)


def bell_draw(rng, shape, scale, most, pieces=(), kind=jnp.bfloat16):
    level = level_of(rng, shape, pieces, -0.22, 0.18) if pieces else 1.0
    values = jax.random.normal(rng, shape, jnp.float32) * scale * level
    return jnp.minimum(jnp.maximum(values, -most), most).astype(kind)


def setup_inputs(seed: int = 0) -> dict:
    arg_keys = jax.random.split(jax.random.key(seed), 8)
    exposure = bell_draw(arg_keys[0], (EXPROWS, W), 1.0, 6.0, ((0, 512),), jnp.float32)
    slots_keys = jax.random.split(jax.random.fold_in(arg_keys[1], 1), EXPROWS // E_DEV)
    slots_turns = jax.random.permutation(jax.random.fold_in(arg_keys[1], 3), EXPROWS // E_DEV)
    slots = jax.vmap(lambda own, number: assign_block(jax.random.fold_in(arg_keys[1], 2), own, number, E_DEV, 2 * SPAN + 1, 1, CAP, 2))(slots_keys, slots_turns).reshape((EXPROWS, 1))
    target_rows = plant(jax.random.randint(arg_keys[2], (EXPROWS,), 0, PR), jax.random.fold_in(arg_keys[2], 1), 0, PR - 1).astype(jnp.int32)
    template = bell_draw(arg_keys[3], (NROWS, NCOLS), 1.0, 6.0, ((0, 8), (1, 64)))
    row_taps = bell_draw(arg_keys[4], (K, TAPS), TAPS ** -0.5, 1.25)
    col_taps = bell_draw(arg_keys[5], (K, TAPS), TAPS ** -0.5, 1.25)
    coef = bell_draw(arg_keys[6], (K, TERMS), 0.1, 0.6, (), jnp.float32)
    return {"exposure": exposure, "slots": slots, "target_rows": target_rows, "template": template, "row_taps": row_taps, "col_taps": col_taps, "coef": coef}


def reference(exposure, slots, target_rows, template, row_taps, col_taps, coef):
    block = (jnp.arange(EXPROWS, dtype=jnp.int32) // E_DEV).astype(jnp.int32)
    ra_place = block // N_DEC
    dec_place = block % N_DEC
    patch = (ra_place + slots[:, 0] - SPAN) % N_RA
    grid = jnp.zeros((N_DEC, PR, N_RA, W), jnp.float32)
    grid = grid.at[dec_place, target_rows, patch].add(exposure)
    science = grid.reshape(NROWS, NCOLS)
    widened = jnp.pad(template.astype(jnp.float32), ((HALF, HALF), (0, 0)))
    widened = jnp.concatenate([widened[:, -HALF:], widened, widened[:, :HALF]], axis=1)
    rows_y = jnp.arange(NROWS, dtype=jnp.int32)
    level = ((2 * rows_y + 1).astype(jnp.float32) / NROWS - 1.0)[:, None]
    cols_x = jnp.arange(NCOLS, dtype=jnp.int32)
    phase = ((2 * cols_x + 1).astype(jnp.float32) * (math.pi / NCOLS))[None, :]
    cosine = jnp.cos(phase)
    sine = jnp.sin(phase)
    upper = row_taps.astype(jnp.float32)
    lower = col_taps.astype(jnp.float32)

    def per_basis(total, inputs):
        utaps, vtaps, terms = inputs
        row_pass = jnp.zeros((NROWS + 2 * HALF, NCOLS), jnp.float32)
        for q in range(TAPS):
            row_pass = row_pass + utaps[q] * widened[:, q:q + NCOLS]
        row_pass = row_pass.astype(jnp.bfloat16).astype(jnp.float32)
        col_pass = jnp.zeros((NROWS, NCOLS), jnp.float32)
        for p in range(TAPS):
            col_pass = col_pass + vtaps[p] * row_pass[p:p + NROWS]
        field = terms[0] + terms[1] * level + terms[2] * (level * level) + terms[3] * cosine + terms[4] * sine + terms[5] * (level * cosine)
        return total + field * col_pass, None

    matched, unused = lax.scan(per_basis, jnp.zeros((NROWS, NCOLS), jnp.float32), (upper, lower, coef))
    return science - matched
```

```python
import functools
import math

import jax
import jax.numpy as jnp
from jax import lax
from jax.experimental import pallas as pl
from jax.experimental.pallas import tpu as pltpu
from jax.sharding import PartitionSpec as P

SPAN = 2
HALF = 10
TILE = 128
WIN = 256
ROWS_PAD = 96


def shifted(value, axis, by):
    length = lax.axis_size(axis)
    return lax.ppermute(value, axis, [(i, (i + by) % length) for i in range(length)])


def extended(value, sides, width, wrap):
    for axis, dim in sides:
        size, length = (lax.axis_size(axis), value.shape[dim])
        up = [(i, (i + 1) % size) for i in range(size if wrap else size - 1)]
        down = [(j, i) for i, j in up]
        last = lax.slice_in_dim(value, length - width, length, axis=dim)
        initial = lax.slice_in_dim(value, 0, width, axis=dim)
        before = lax.ppermute(last, axis, up)
        after = lax.ppermute(initial, axis, down)
        value = jnp.concatenate([before, value, after], axis=dim)
    return value


def row_band(row_taps, n_basis):
    taps = row_taps.shape[1]
    offset = jnp.arange(WIN, dtype=jnp.int32)[:, None] - jnp.arange(TILE, dtype=jnp.int32)[None, :]
    picks = (offset[None, :, :] == jnp.arange(taps, dtype=jnp.int32)[:, None, None]).astype(jnp.float32)
    band = jnp.einsum("kq,qct->ckt", row_taps.astype(jnp.float32), picks)
    band = jnp.pad(band, ((0, 0), (0, n_basis - row_taps.shape[0]), (0, 0)))
    return band.reshape(WIN, n_basis * TILE).astype(jnp.bfloat16)


def field_band(col_taps, coef, level, n_basis):
    k_count, taps = col_taps.shape
    p_rows = level.shape[0]
    offset = jnp.arange(ROWS_PAD, dtype=jnp.int32)[None, :] - jnp.arange(p_rows, dtype=jnp.int32)[:, None]
    picks = (offset[None, :, :] == jnp.arange(taps, dtype=jnp.int32)[:, None, None]).astype(jnp.float32)
    shifted_taps = jnp.einsum("kp,pyr->kyr", col_taps.astype(jnp.float32), picks)
    lv = level[None, :]
    plain = coef[:, 0, None] + coef[:, 1, None] * lv + coef[:, 2, None] * (lv * lv)
    with_cos = coef[:, 3, None] + coef[:, 5, None] * lv
    with_sin = jnp.broadcast_to(coef[:, 4, None], plain.shape)
    scale = jnp.stack([plain, with_cos, with_sin])
    weights = scale[:, :, :, None] * shifted_taps[None]
    weights = jnp.transpose(weights, (0, 2, 1, 3))
    weights = jnp.pad(weights, ((0, 0), (0, 0), (0, n_basis - k_count), (0, 0)))
    weights = weights.reshape(3 * p_rows, n_basis * ROWS_PAD)
    high = weights.astype(jnp.bfloat16)
    low = (weights - high.astype(jnp.float32)).astype(jnp.bfloat16)
    return jnp.concatenate([high, low], axis=0)


def conv_kernel(n_tiles, n_basis, p_rows, windows_ref, band_ref, weights_ref, trig_ref, out_ref, rp_ref):
    pair = 2 * TILE

    def row_step(step, carry):
        col = pl.multiple_of(step * pair, pair)
        part = jnp.dot(windows_ref[...], band_ref[:, pl.ds(col, pair)], preferred_element_type=jnp.float32)
        part = part.astype(jnp.bfloat16)
        for half in range(2):
            base = pl.multiple_of((2 * step + half) * ROWS_PAD, ROWS_PAD)
            for t in range(n_tiles):
                rp_ref[pl.ds(base, ROWS_PAD), t * TILE:(t + 1) * TILE] = part[
                    t * ROWS_PAD:(t + 1) * ROWS_PAD, half * TILE:(half + 1) * TILE
                ]
        return carry

    lax.fori_loop(0, n_basis // 2, row_step, 0)

    chunk = 256

    def col_step(step, carry):
        col = pl.multiple_of(step * chunk, chunk)
        sums = jnp.dot(weights_ref[...], rp_ref[:, pl.ds(col, chunk)], preferred_element_type=jnp.float32)
        lo = 3 * p_rows
        plain = sums[0:p_rows] + sums[lo:lo + p_rows]
        with_cos = sums[p_rows:2 * p_rows] + sums[lo + p_rows:lo + 2 * p_rows]
        with_sin = sums[2 * p_rows:3 * p_rows] + sums[lo + 2 * p_rows:lo + 3 * p_rows]
        cosine = trig_ref[0:1, pl.ds(col, chunk)]
        sine = trig_ref[1:2, pl.ds(col, chunk)]
        out_ref[:, pl.ds(col, chunk)] = plain + cosine * with_cos + sine * with_sin
        return carry

    lax.fori_loop(0, out_ref.shape[1] // chunk, col_step, 0)


def matched_template(padded, row_taps, col_taps, coef, level, trig):
    p_rows = level.shape[0]
    width = trig.shape[1]
    n_tiles = width // TILE
    n_basis = row_taps.shape[0] + (row_taps.shape[0] % 2)
    padded = jnp.pad(padded, ((0, ROWS_PAD - padded.shape[0]), (0, n_tiles * TILE + WIN - TILE - padded.shape[1])))
    windows = jnp.stack([padded[:, t * TILE:t * TILE + WIN] for t in range(n_tiles)]).reshape(n_tiles * ROWS_PAD, WIN)
    band = row_band(row_taps, n_basis)
    weights = field_band(col_taps, coef, level, n_basis)
    flops = 2 * n_tiles * ROWS_PAD * WIN * n_basis * TILE + 2 * weights.shape[0] * weights.shape[1] * width
    return pl.pallas_call(
        functools.partial(conv_kernel, n_tiles, n_basis, p_rows),
        out_shape=jax.ShapeDtypeStruct((p_rows, width), jnp.float32),
        in_specs=[pl.BlockSpec(memory_space=pltpu.VMEM)] * 4,
        out_specs=pl.BlockSpec(memory_space=pltpu.VMEM),
        scratch_shapes=[pltpu.VMEM((n_basis * ROWS_PAD, width), jnp.bfloat16)],
        compiler_params=pltpu.CompilerParams(vmem_limit_bytes=60 * 1024 * 1024),
        cost_estimate=pl.CostEstimate(flops=flops, transcendentals=0, bytes_accessed=8 * 1024 * 1024),
    )(windows, band, weights, trig)


def local(exposure, slots, target_rows, template, row_taps, col_taps, coef):
    e_rows, width = exposure.shape
    p_rows = template.shape[0]
    n_slots = 2 * SPAN + 1
    slot_ids = slots[:, 0]
    flat_place = slot_ids * p_rows + target_rows
    select = (jnp.arange(n_slots * p_rows, dtype=jnp.int32)[:, None] == flat_place[None, :]).astype(jnp.float32)
    partial = jnp.dot(
        select, exposure, precision=lax.Precision.HIGHEST, preferred_element_type=jnp.float32
    ).reshape(n_slots, p_rows, width)
    arrived = [partial[SPAN]]
    for offset in range(-SPAN, SPAN + 1):
        if offset != 0:
            arrived.append(shifted(partial[SPAN + offset], "ra", offset))

    widened = extended(template, (("ra", 1),), HALF, True)
    padded = extended(widened, (("dec", 0),), HALF, False)

    total_rows = p_rows * lax.axis_size("dec")
    total_cols = width * lax.axis_size("ra")
    rows_y = lax.axis_index("dec") * p_rows + jnp.arange(p_rows, dtype=jnp.int32)
    level = (2 * rows_y + 1).astype(jnp.float32) / total_rows - 1.0
    cols_x = lax.axis_index("ra") * width + jnp.arange(width, dtype=jnp.int32)
    phase = (2 * cols_x + 1).astype(jnp.float32) * (math.pi / total_cols)
    trig = jnp.stack([jnp.cos(phase), jnp.sin(phase)])

    matched = matched_template(padded, row_taps, col_taps, coef, level, trig)
    science = arrived[0]
    for part in arrived[1:]:
        science = science + part
    return science - matched


def solution(mesh):
    return jax.shard_map(
        local,
        mesh=mesh,
        in_specs=(
            P(("ra", "dec"), None),
            P(("ra", "dec"), None),
            P(("ra", "dec")),
            P("dec", "ra"),
            P(),
            P(),
            P(),
        ),
        out_specs=P("dec", "ra"),
        check_vma=False,
    )
```

```python
import functools
import math

import jax
import jax.numpy as jnp
from jax import lax
from jax.experimental import pallas as pl
from jax.experimental.pallas import tpu as pltpu
from jax.sharding import PartitionSpec as P

SPAN = 2
HALF = 10
TILE = 128
WIN = 256
ROWS_PAD = 96


def shifted(value, axis, by):
    length = lax.axis_size(axis)
    return lax.ppermute(value, axis, [(i, (i + by) % length) for i in range(length)])


def extended(value, sides, width, wrap):
    for axis, dim in sides:
        size, length = (lax.axis_size(axis), value.shape[dim])
        up = [(i, (i + 1) % size) for i in range(size if wrap else size - 1)]
        down = [(j, i) for i, j in up]
        last = lax.slice_in_dim(value, length - width, length, axis=dim)
        initial = lax.slice_in_dim(value, 0, width, axis=dim)
        before = lax.ppermute(last, axis, up)
        after = lax.ppermute(initial, axis, down)
        value = jnp.concatenate([before, value, after], axis=dim)
    return value


def row_band(row_taps, n_basis):
    taps = row_taps.shape[1]
    offset = jnp.arange(WIN, dtype=jnp.int32)[:, None] - jnp.arange(TILE, dtype=jnp.int32)[None, :]
    picks = (offset[None, :, :] == jnp.arange(taps, dtype=jnp.int32)[:, None, None]).astype(jnp.bfloat16)
    padded_taps = jnp.pad(row_taps, ((0, n_basis - row_taps.shape[0]), (0, 0)))
    band = jnp.dot(padded_taps, picks.reshape(taps, WIN * TILE), preferred_element_type=jnp.float32)
    return band.astype(jnp.bfloat16).reshape(n_basis, WIN, TILE)


def field_band(col_taps, coef, level, n_basis):
    k_count, taps = col_taps.shape
    p_rows = level.shape[0]
    offset = jnp.arange(ROWS_PAD, dtype=jnp.int32)[None, :] - jnp.arange(p_rows, dtype=jnp.int32)[:, None]
    picks = (offset[:, None, :] == jnp.arange(taps, dtype=jnp.int32)[None, :, None]).astype(jnp.float32)
    taps_f = jnp.pad(col_taps.astype(jnp.float32), ((0, n_basis - k_count), (0, 0)))
    shifted_taps = jnp.einsum("kp,ypr->ykr", taps_f, picks)
    coef = jnp.pad(coef, ((0, n_basis - k_count), (0, 0)))
    lv = level[:, None]
    plain = coef[None, :, 0] + coef[None, :, 1] * lv + coef[None, :, 2] * (lv * lv)
    with_cos = coef[None, :, 3] + coef[None, :, 5] * lv
    with_sin = jnp.broadcast_to(coef[None, :, 4], plain.shape)
    scale = jnp.stack([plain, with_cos, with_sin])
    weights = (scale[:, :, :, None] * shifted_taps[None]).reshape(3 * p_rows, n_basis * ROWS_PAD)
    high = lax.reduce_precision(weights, exponent_bits=8, mantissa_bits=7)
    low = weights - high
    return jnp.concatenate([high.astype(jnp.bfloat16), low.astype(jnp.bfloat16)], axis=0)


def conv_kernel(n_tiles, n_basis, p_rows, padded_ref, band_ref, weights_ref, trig_ref, out_ref, rp_ref, windows_ref):
    for t in range(n_tiles):
        windows_ref[t * ROWS_PAD:(t + 1) * ROWS_PAD, :] = padded_ref[:, t * TILE:t * TILE + WIN]

    def row_step(step, carry):
        rhs = jnp.concatenate([band_ref[2 * step], band_ref[2 * step + 1]], axis=1)
        part = jnp.dot(windows_ref[...], rhs, preferred_element_type=jnp.float32)
        part = part.astype(jnp.bfloat16)
        for half in range(2):
            base = pl.multiple_of((2 * step + half) * ROWS_PAD, ROWS_PAD)
            for t in range(n_tiles):
                rp_ref[pl.ds(base, ROWS_PAD), t * TILE:(t + 1) * TILE] = part[
                    t * ROWS_PAD:(t + 1) * ROWS_PAD, half * TILE:(half + 1) * TILE
                ]
        return carry

    lax.fori_loop(0, n_basis // 2, row_step, 0)

    chunk = 256

    def col_step(step, carry):
        col = pl.multiple_of(step * chunk, chunk)
        sums = jnp.dot(weights_ref[...], rp_ref[:, pl.ds(col, chunk)], preferred_element_type=jnp.float32)
        lo = 3 * p_rows
        plain = sums[0:p_rows] + sums[lo:lo + p_rows]
        with_cos = sums[p_rows:2 * p_rows] + sums[lo + p_rows:lo + 2 * p_rows]
        with_sin = sums[2 * p_rows:3 * p_rows] + sums[lo + 2 * p_rows:lo + 3 * p_rows]
        cosine = trig_ref[0:1, pl.ds(col, chunk)]
        sine = trig_ref[1:2, pl.ds(col, chunk)]
        out_ref[:, pl.ds(col, chunk)] = plain + cosine * with_cos + sine * with_sin
        return carry

    lax.fori_loop(0, out_ref.shape[1] // chunk, col_step, 0)


def matched_template(padded, row_taps, col_taps, coef, level, trig):
    p_rows = level.shape[0]
    width = trig.shape[1]
    n_tiles = width // TILE
    n_basis = row_taps.shape[0] + (row_taps.shape[0] % 2)
    padded = jnp.pad(padded, ((0, ROWS_PAD - padded.shape[0]), (0, n_tiles * TILE + WIN - TILE - padded.shape[1])))
    band = row_band(row_taps, n_basis)
    weights = field_band(col_taps, coef, level, n_basis)
    flops = 2 * n_tiles * ROWS_PAD * WIN * n_basis * TILE + 2 * weights.shape[0] * weights.shape[1] * width
    return pl.pallas_call(
        functools.partial(conv_kernel, n_tiles, n_basis, p_rows),
        out_shape=jax.ShapeDtypeStruct((p_rows, width), jnp.float32),
        in_specs=[pl.BlockSpec(memory_space=pltpu.VMEM)] * 4,
        out_specs=pl.BlockSpec(memory_space=pltpu.VMEM),
        scratch_shapes=[
            pltpu.VMEM((n_basis * ROWS_PAD, width), jnp.bfloat16),
            pltpu.VMEM((n_tiles * ROWS_PAD, WIN), jnp.bfloat16),
        ],
        compiler_params=pltpu.CompilerParams(vmem_limit_bytes=60 * 1024 * 1024),
        cost_estimate=pl.CostEstimate(flops=flops, transcendentals=0, bytes_accessed=8 * 1024 * 1024),
    )(padded, band, weights, trig)


def local(exposure, slots, target_rows, template, row_taps, col_taps, coef):
    e_rows, width = exposure.shape
    p_rows = template.shape[0]
    n_slots = 2 * SPAN + 1
    slot_ids = slots[:, 0]
    flat_place = slot_ids * p_rows + target_rows
    select = (jnp.arange(n_slots * p_rows, dtype=jnp.int32)[:, None] == flat_place[None, :]).astype(jnp.float32)
    partial = jnp.dot(
        select, exposure, precision=lax.Precision.HIGHEST, preferred_element_type=jnp.float32
    ).reshape(n_slots, p_rows, width)
    arrived = [partial[SPAN]]
    for offset in range(-SPAN, SPAN + 1):
        if offset != 0:
            arrived.append(shifted(partial[SPAN + offset], "ra", offset))

    widened = extended(template, (("ra", 1),), HALF, True)
    padded = extended(widened, (("dec", 0),), HALF, False)

    total_rows = p_rows * lax.axis_size("dec")
    total_cols = width * lax.axis_size("ra")
    rows_y = lax.axis_index("dec") * p_rows + jnp.arange(p_rows, dtype=jnp.int32)
    level = (2 * rows_y + 1).astype(jnp.float32) / total_rows - 1.0
    cols_x = lax.axis_index("ra") * width + jnp.arange(width, dtype=jnp.int32)
    phase = (2 * cols_x + 1).astype(jnp.float32) * (math.pi / total_cols)
    trig = jnp.stack([jnp.cos(phase), jnp.sin(phase)])

    matched = matched_template(padded, row_taps, col_taps, coef, level, trig)
    science = arrived[0]
    for part in arrived[1:]:
        science = science + part
    return science - matched


def solution(mesh):
    return jax.shard_map(
        local,
        mesh=mesh,
        in_specs=(
            P(("ra", "dec"), None),
            P(("ra", "dec"), None),
            P(("ra", "dec")),
            P("dec", "ra"),
            P(),
            P(),
            P(),
        ),
        out_specs=P("dec", "ra"),
        check_vma=False,
    )
```

```python
import functools
import math

import jax
import jax.numpy as jnp
from jax import lax
from jax.experimental import pallas as pl
from jax.experimental.pallas import tpu as pltpu
from jax.sharding import PartitionSpec as P

SPAN = 2
HALF = 10
TILE = 128
WIN = 256
ROWS_PAD = 96
BLOCK = 128


def shifted(value, axis, by):
    length = lax.axis_size(axis)
    return lax.ppermute(value, axis, [(i, (i + by) % length) for i in range(length)])


def extended(value, sides, width, wrap):
    for axis, dim in sides:
        size, length = (lax.axis_size(axis), value.shape[dim])
        up = [(i, (i + 1) % size) for i in range(size if wrap else size - 1)]
        down = [(j, i) for i, j in up]
        last = lax.slice_in_dim(value, length - width, length, axis=dim)
        initial = lax.slice_in_dim(value, 0, width, axis=dim)
        before = lax.ppermute(last, axis, up)
        after = lax.ppermute(initial, axis, down)
        value = jnp.concatenate([before, value, after], axis=dim)
    return value


def conv_kernel(n_tiles, n_basis, p_rows, coef_ref, utaps_ref, vtaps_ref, level_ref, trig_ref, padded_ref,
                out_ref, rp_ref, windows_ref, weights_ref):
    f32, bf16 = jnp.float32, jnp.bfloat16
    for t in range(n_tiles):
        windows_ref[t * ROWS_PAD:(t + 1) * ROWS_PAD, :] = padded_ref[:, t * TILE:t * TILE + WIN]

    level = level_ref[...]
    level_sq = level * level

    def weight_step(k, carry):
        vrow = jnp.broadcast_to(vtaps_ref[pl.ds(k, 1), :], (p_rows, BLOCK))
        shifted_taps = pltpu.roll(vrow, 0, 1, stride=1, stride_axis=0)
        plain = coef_ref[k, 0] + coef_ref[k, 1] * level + coef_ref[k, 2] * level_sq
        with_cos = coef_ref[k, 3] + coef_ref[k, 5] * level
        col = pl.multiple_of(k * BLOCK, BLOCK)
        for term, scale in enumerate((plain, with_cos, coef_ref[k, 4])):
            w = scale * shifted_taps
            high = w.astype(bf16)
            low = (w - high.astype(f32)).astype(bf16)
            weights_ref[term * p_rows:(term + 1) * p_rows, pl.ds(col, BLOCK)] = high
            weights_ref[(3 + term) * p_rows:(4 + term) * p_rows, pl.ds(col, BLOCK)] = low
        rp_ref[pl.ds(k * BLOCK + ROWS_PAD, BLOCK - ROWS_PAD), :] = jnp.zeros(
            (BLOCK - ROWS_PAD, rp_ref.shape[1]), bf16
        )
        return carry

    lax.fori_loop(0, n_basis, weight_step, 0)

    def row_step(step, carry):
        bands = []
        for half in range(2):
            urow = jnp.broadcast_to(utaps_ref[pl.ds(2 * step + half, 1), :], (TILE, WIN))
            bands.append(pltpu.roll(urow, 0, 1, stride=1, stride_axis=0))
        band_t = jnp.concatenate(bands, axis=0).astype(bf16)
        part = lax.dot_general(
            windows_ref[...], band_t, (((1,), (1,)), ((), ())), preferred_element_type=f32
        ).astype(bf16)
        for half in range(2):
            base = pl.multiple_of((2 * step + half) * BLOCK, BLOCK)
            for t in range(n_tiles):
                rp_ref[pl.ds(base, ROWS_PAD), t * TILE:(t + 1) * TILE] = part[
                    t * ROWS_PAD:(t + 1) * ROWS_PAD, half * TILE:(half + 1) * TILE
                ]
        return carry

    lax.fori_loop(0, n_basis // 2, row_step, 0)

    chunk = 256

    def col_step(step, carry):
        col = pl.multiple_of(step * chunk, chunk)
        sums = jnp.dot(weights_ref[...], rp_ref[:, pl.ds(col, chunk)], preferred_element_type=f32)
        lo = 3 * p_rows
        plain = sums[0:p_rows] + sums[lo:lo + p_rows]
        with_cos = sums[p_rows:2 * p_rows] + sums[lo + p_rows:lo + 2 * p_rows]
        with_sin = sums[2 * p_rows:3 * p_rows] + sums[lo + 2 * p_rows:lo + 3 * p_rows]
        cosine = trig_ref[0:1, pl.ds(col, chunk)]
        sine = trig_ref[1:2, pl.ds(col, chunk)]
        out_ref[:, pl.ds(col, chunk)] = plain + cosine * with_cos + sine * with_sin
        return carry

    lax.fori_loop(0, out_ref.shape[1] // chunk, col_step, 0)


def matched_template(padded, row_taps, col_taps, coef, level, trig):
    p_rows = level.shape[0]
    width = trig.shape[1]
    n_tiles = width // TILE
    k_count = row_taps.shape[0]
    n_basis = k_count + (k_count % 2)
    padded = jnp.pad(padded, ((0, ROWS_PAD - padded.shape[0]), (0, n_tiles * TILE + WIN - TILE - padded.shape[1])))
    utaps = jnp.pad(row_taps.astype(jnp.float32), ((0, n_basis - k_count), (0, WIN - row_taps.shape[1])))
    vtaps = jnp.pad(col_taps.astype(jnp.float32), ((0, n_basis - k_count), (0, BLOCK - col_taps.shape[1])))
    coef = jnp.pad(coef, ((0, n_basis - k_count), (0, 0)))
    level = jnp.broadcast_to(level[:, None], (p_rows, BLOCK))
    flops = 2 * n_tiles * ROWS_PAD * WIN * n_basis * TILE + 2 * 6 * p_rows * n_basis * BLOCK * width
    vmem = pl.BlockSpec(memory_space=pltpu.VMEM)
    return pl.pallas_call(
        functools.partial(conv_kernel, n_tiles, n_basis, p_rows),
        out_shape=jax.ShapeDtypeStruct((p_rows, width), jnp.float32),
        in_specs=[pl.BlockSpec(memory_space=pltpu.SMEM)] + [vmem] * 5,
        out_specs=vmem,
        scratch_shapes=[
            pltpu.VMEM((n_basis * BLOCK, width), jnp.bfloat16),
            pltpu.VMEM((n_tiles * ROWS_PAD, WIN), jnp.bfloat16),
            pltpu.VMEM((6 * p_rows, n_basis * BLOCK), jnp.bfloat16),
        ],
        compiler_params=pltpu.CompilerParams(vmem_limit_bytes=60 * 1024 * 1024),
        cost_estimate=pl.CostEstimate(flops=flops, transcendentals=0, bytes_accessed=4 * 1024 * 1024),
    )(coef, utaps, vtaps, level, trig, padded)


def local(exposure, slots, target_rows, template, row_taps, col_taps, coef):
    e_rows, width = exposure.shape
    p_rows = template.shape[0]
    n_slots = 2 * SPAN + 1
    slot_ids = slots[:, 0]
    flat_place = slot_ids * p_rows + target_rows
    select = (jnp.arange(n_slots * p_rows, dtype=jnp.int32)[:, None] == flat_place[None, :]).astype(jnp.float32)
    partial = jnp.dot(
        select, exposure, precision=lax.Precision.HIGHEST, preferred_element_type=jnp.float32
    ).reshape(n_slots, p_rows, width)
    arrived = [partial[SPAN]]
    for offset in range(-SPAN, SPAN + 1):
        if offset != 0:
            arrived.append(shifted(partial[SPAN + offset], "ra", offset))

    widened = extended(template, (("ra", 1),), HALF, True)
    padded = extended(widened, (("dec", 0),), HALF, False)

    total_rows = p_rows * lax.axis_size("dec")
    total_cols = width * lax.axis_size("ra")
    rows_y = lax.axis_index("dec") * p_rows + jnp.arange(p_rows, dtype=jnp.int32)
    level = (2 * rows_y + 1).astype(jnp.float32) / total_rows - 1.0
    cols_x = lax.axis_index("ra") * width + jnp.arange(width, dtype=jnp.int32)
    phase = (2 * cols_x + 1).astype(jnp.float32) * (math.pi / total_cols)
    trig = jnp.stack([jnp.cos(phase), jnp.sin(phase)])

    matched = matched_template(padded, row_taps, col_taps, coef, level, trig)
    science = arrived[0]
    for part in arrived[1:]:
        science = science + part
    return science - matched


def solution(mesh):
    return jax.shard_map(
        local,
        mesh=mesh,
        in_specs=(
            P(("ra", "dec"), None),
            P(("ra", "dec"), None),
            P(("ra", "dec")),
            P("dec", "ra"),
            P(),
            P(),
            P(),
        ),
        out_specs=P("dec", "ra"),
        check_vma=False,
    )
```

```python
import functools
import math

import jax
import jax.numpy as jnp
from jax import lax
from jax.experimental import pallas as pl
from jax.experimental.pallas import tpu as pltpu
from jax.sharding import PartitionSpec as P

SPAN = 2
HALF = 10
TILE = 128
WIN = 256
ROWS_PAD = 96
BLOCK = 128
EDGE = 16
MESH = pl.DeviceIdType.MESH


def conv_kernel(n_tiles, n_basis, p_rows, coef_ref, utaps_ref, vtaps_ref, level_ref, trig_ref, template_ref,
                grid_ref, out_ref, rp_ref, windows_ref, weights_ref, ext_ref, arrived_ref,
                halo_send, halo_recv, grid_send, grid_recv):
    f32, bf16 = jnp.float32, jnp.bfloat16
    n_ra, n_dec = lax.axis_size("ra"), lax.axis_size("dec")
    ra, dec = lax.axis_index("ra"), lax.axis_index("dec")

    def peer(d_ra, d_dec):
        return (lax.rem(ra + d_ra + n_ra, n_ra), lax.rem(dec + d_dec + n_dec, n_dec))

    width = template_ref.shape[1]
    ext_ref[EDGE:EDGE + p_rows, TILE:TILE + width] = template_ref[...]
    partners = [(1, 0), (-1, 0), (2, 0), (-2, 0), (0, 1), (0, -1), (1, 1), (1, -1), (-1, 1), (-1, -1)]
    barrier = pltpu.get_barrier_semaphore()
    for d_ra, d_dec in partners:
        pl.semaphore_signal(barrier, inc=1, device_id=peer(d_ra, d_dec), device_id_type=MESH)
    pl.semaphore_wait(barrier, len(partners))

    top, bottom = slice(p_rows - EDGE, p_rows), slice(0, EDGE)
    left, right = slice(width - TILE, width), slice(0, TILE)
    all_rows, all_cols = slice(0, p_rows), slice(0, width)
    inner_rows, inner_cols = slice(EDGE, EDGE + p_rows), slice(TILE, TILE + width)
    low_rows, high_cols = slice(EDGE + p_rows, 2 * EDGE + p_rows), slice(TILE + width, 2 * TILE + width)
    pieces = [
        ((-1, 0), all_rows, left, inner_rows, slice(0, TILE)),
        ((1, 0), all_rows, right, inner_rows, high_cols),
        ((0, -1), top, all_cols, slice(0, EDGE), inner_cols),
        ((0, 1), bottom, all_cols, low_rows, inner_cols),
        ((-1, -1), top, left, slice(0, EDGE), slice(0, TILE)),
        ((1, -1), top, right, slice(0, EDGE), high_cols),
        ((-1, 1), bottom, left, low_rows, slice(0, TILE)),
        ((1, 1), bottom, right, low_rows, high_cols),
    ]
    halo_copies = []
    for n, ((s_ra, s_dec), my_rows, my_cols, rows, cols) in enumerate(pieces):
        copy = pltpu.make_async_remote_copy(
            src_ref=template_ref.at[my_rows, my_cols],
            dst_ref=ext_ref.at[rows, cols],
            send_sem=halo_send.at[n],
            recv_sem=halo_recv.at[n],
            device_id=peer(-s_ra, -s_dec),
            device_id_type=MESH,
        )
        copy.start()
        halo_copies.append(copy)
    grid_copies = []
    for m, slot in enumerate([s for s in range(2 * SPAN + 1) if s != SPAN]):
        copy = pltpu.make_async_remote_copy(
            src_ref=grid_ref.at[slot],
            dst_ref=arrived_ref.at[m],
            send_sem=grid_send.at[m],
            recv_sem=grid_recv.at[m],
            device_id=peer(slot - SPAN, 0),
            device_id_type=MESH,
        )
        copy.start()
        grid_copies.append(copy)

    level = level_ref[...]
    level_sq = level * level

    def weight_step(k, carry):
        vrow = jnp.broadcast_to(vtaps_ref[pl.ds(k, 1), :], (p_rows, BLOCK))
        shifted_taps = pltpu.roll(vrow, EDGE - HALF, 1, stride=1, stride_axis=0)
        plain = coef_ref[k, 0] + coef_ref[k, 1] * level + coef_ref[k, 2] * level_sq
        with_cos = coef_ref[k, 3] + coef_ref[k, 5] * level
        col = pl.multiple_of(k * BLOCK, BLOCK)
        for term, scale in enumerate((plain, with_cos, coef_ref[k, 4])):
            w = scale * shifted_taps
            high = w.astype(bf16)
            low = (w - high.astype(f32)).astype(bf16)
            weights_ref[term * p_rows:(term + 1) * p_rows, pl.ds(col, BLOCK)] = high
            weights_ref[(3 + term) * p_rows:(4 + term) * p_rows, pl.ds(col, BLOCK)] = low
        rp_ref[pl.ds(k * BLOCK + ROWS_PAD, BLOCK - ROWS_PAD), :] = jnp.zeros(
            (BLOCK - ROWS_PAD, rp_ref.shape[1]), bf16
        )
        return carry

    lax.fori_loop(0, n_basis, weight_step, 0)

    for copy in halo_copies:
        copy.wait()
    keep_top = dec > 0
    keep_bottom = dec < n_dec - 1
    ext_ref[0:EDGE, :] = jnp.where(keep_top, ext_ref[0:EDGE, :], jnp.zeros_like(ext_ref[0:EDGE, :]))
    ext_ref[EDGE + p_rows:, :] = jnp.where(
        keep_bottom, ext_ref[EDGE + p_rows:, :], jnp.zeros_like(ext_ref[EDGE + p_rows:, :])
    )
    for t in range(n_tiles):
        slab = ext_ref[:, t * TILE:t * TILE + 3 * TILE].astype(f32)
        slab = pltpu.roll(slab, 3 * TILE - (TILE - HALF), 1)
        windows_ref[t * ROWS_PAD:(t + 1) * ROWS_PAD, :] = slab[:, 0:WIN].astype(bf16)

    def row_step(step, carry):
        bands = []
        for half in range(2):
            urow = jnp.broadcast_to(utaps_ref[pl.ds(2 * step + half, 1), :], (TILE, WIN))
            bands.append(pltpu.roll(urow, 0, 1, stride=1, stride_axis=0))
        band_t = jnp.concatenate(bands, axis=0).astype(bf16)
        part = lax.dot_general(
            windows_ref[...], band_t, (((1,), (1,)), ((), ())), preferred_element_type=f32
        ).astype(bf16)
        for half in range(2):
            base = pl.multiple_of((2 * step + half) * BLOCK, BLOCK)
            for t in range(n_tiles):
                rp_ref[pl.ds(base, ROWS_PAD), t * TILE:(t + 1) * TILE] = part[
                    t * ROWS_PAD:(t + 1) * ROWS_PAD, half * TILE:(half + 1) * TILE
                ]
        return carry

    lax.fori_loop(0, n_basis // 2, row_step, 0)

    chunk = 256

    def col_step(step, carry):
        col = pl.multiple_of(step * chunk, chunk)
        sums = jnp.dot(weights_ref[...], rp_ref[:, pl.ds(col, chunk)], preferred_element_type=f32)
        lo = 3 * p_rows
        plain = sums[0:p_rows] + sums[lo:lo + p_rows]
        with_cos = sums[p_rows:2 * p_rows] + sums[lo + p_rows:lo + 2 * p_rows]
        with_sin = sums[2 * p_rows:3 * p_rows] + sums[lo + 2 * p_rows:lo + 3 * p_rows]
        cosine = trig_ref[0:1, pl.ds(col, chunk)]
        sine = trig_ref[1:2, pl.ds(col, chunk)]
        out_ref[:, pl.ds(col, chunk)] = plain + cosine * with_cos + sine * with_sin
        return carry

    lax.fori_loop(0, out_ref.shape[1] // chunk, col_step, 0)

    for copy in grid_copies:
        copy.wait()
    science = grid_ref[SPAN]
    for m in range(len(grid_copies)):
        science = science + arrived_ref[m]
    out_ref[...] = science - out_ref[...]


def difference_image(template, grid, row_taps, col_taps, coef, level, trig):
    p_rows = level.shape[0]
    width = trig.shape[1]
    n_tiles = width // TILE
    k_count = row_taps.shape[0]
    n_basis = k_count + (k_count % 2)
    utaps = jnp.pad(row_taps.astype(jnp.float32), ((0, n_basis - k_count), (0, WIN - row_taps.shape[1])))
    vtaps = jnp.pad(col_taps.astype(jnp.float32), ((0, n_basis - k_count), (0, BLOCK - col_taps.shape[1])))
    coef = jnp.pad(coef, ((0, n_basis - k_count), (0, 0)))
    level = jnp.broadcast_to(level[:, None], (p_rows, BLOCK))
    flops = 2 * n_tiles * ROWS_PAD * WIN * n_basis * TILE + 2 * 6 * p_rows * n_basis * BLOCK * width
    vmem = pl.BlockSpec(memory_space=pltpu.VMEM)
    n_out = 2 * SPAN
    return pl.pallas_call(
        functools.partial(conv_kernel, n_tiles, n_basis, p_rows),
        out_shape=jax.ShapeDtypeStruct((p_rows, width), jnp.float32),
        in_specs=[pl.BlockSpec(memory_space=pltpu.SMEM)] + [vmem] * 6,
        out_specs=vmem,
        scratch_shapes=[
            pltpu.VMEM((n_basis * BLOCK, width), jnp.bfloat16),
            pltpu.VMEM((n_tiles * ROWS_PAD, WIN), jnp.bfloat16),
            pltpu.VMEM((6 * p_rows, n_basis * BLOCK), jnp.bfloat16),
            pltpu.VMEM((p_rows + 2 * EDGE, width + 2 * TILE), jnp.bfloat16),
            pltpu.VMEM((n_out, p_rows, width), jnp.float32),
            pltpu.SemaphoreType.DMA((8,)),
            pltpu.SemaphoreType.DMA((8,)),
            pltpu.SemaphoreType.DMA((n_out,)),
            pltpu.SemaphoreType.DMA((n_out,)),
        ],
        compiler_params=pltpu.CompilerParams(
            vmem_limit_bytes=60 * 1024 * 1024, collective_id=0, has_side_effects=True
        ),
        cost_estimate=pl.CostEstimate(flops=flops, transcendentals=0, bytes_accessed=8 * 1024 * 1024),
    )(coef, utaps, vtaps, level, trig, template, grid)


def local(exposure, slots, target_rows, template, row_taps, col_taps, coef):
    e_rows, width = exposure.shape
    p_rows = template.shape[0]
    n_slots = 2 * SPAN + 1
    slot_ids = slots[:, 0]
    flat_place = slot_ids * p_rows + target_rows
    select = (jnp.arange(n_slots * p_rows, dtype=jnp.int32)[:, None] == flat_place[None, :]).astype(jnp.float32)
    partial = jnp.dot(
        select, exposure, precision=lax.Precision.HIGHEST, preferred_element_type=jnp.float32
    ).reshape(n_slots, p_rows, width)
    total_rows = p_rows * lax.axis_size("dec")
    total_cols = width * lax.axis_size("ra")
    rows_y = lax.axis_index("dec") * p_rows + jnp.arange(p_rows, dtype=jnp.int32)
    level = (2 * rows_y + 1).astype(jnp.float32) / total_rows - 1.0
    cols_x = lax.axis_index("ra") * width + jnp.arange(width, dtype=jnp.int32)
    phase = (2 * cols_x + 1).astype(jnp.float32) * (math.pi / total_cols)
    trig = jnp.stack([jnp.cos(phase), jnp.sin(phase)])

    return difference_image(template, partial, row_taps, col_taps, coef, level, trig)


def solution(mesh):
    return jax.shard_map(
        local,
        mesh=mesh,
        in_specs=(
            P(("ra", "dec"), None),
            P(("ra", "dec"), None),
            P(("ra", "dec")),
            P("dec", "ra"),
            P(),
            P(),
            P(),
        ),
        out_specs=P("dec", "ra"),
        check_vma=False,
    )
```

```python
import functools
import math

import jax
import jax.numpy as jnp
from jax import lax
from jax.experimental import pallas as pl
from jax.experimental.pallas import tpu as pltpu
from jax.sharding import PartitionSpec as P

SPAN = 2
HALF = 10
TILE = 128
WIN = 256
ROWS_PAD = 96
BLOCK = 128
EDGE = 16
MESH = pl.DeviceIdType.MESH
OWN, MIXED, NEAR, FAR = range(4)


def conv_kernel(n_tiles, n_basis, p_rows, coef_ref, utaps_ref, vtaps_ref, level_ref, trig_ref, template_ref,
                grid_ref, out_ref, rp_ref, windows_ref, weights_ref, ext_ref, arrived_ref, combined_ref,
                halo_send, halo_recv, grid_send, grid_recv):
    f32, bf16 = jnp.float32, jnp.bfloat16
    n_ra, n_dec = lax.axis_size("ra"), lax.axis_size("dec")
    ra, dec = lax.axis_index("ra"), lax.axis_index("dec")

    def peer(d_ra, d_dec):
        return (lax.rem(ra + d_ra + n_ra, n_ra), lax.rem(dec + d_dec + n_dec, n_dec))

    width = template_ref.shape[1]
    ext_ref[EDGE:EDGE + p_rows, TILE:TILE + width] = template_ref[...]
    partners = [(1, 0), (-1, 0), (2, 0), (-2, 0), (0, 1), (0, -1), (1, 1), (1, -1), (-1, 1), (-1, -1)]
    barrier = pltpu.get_barrier_semaphore()
    for d_ra, d_dec in partners:
        pl.semaphore_signal(barrier, inc=1, device_id=peer(d_ra, d_dec), device_id_type=MESH)
    pl.semaphore_wait(barrier, len(partners))

    top, bottom = slice(p_rows - EDGE, p_rows), slice(0, EDGE)
    left, right = slice(width - TILE, width), slice(0, TILE)
    all_rows, all_cols = slice(0, p_rows), slice(0, width)
    inner_rows, inner_cols = slice(EDGE, EDGE + p_rows), slice(TILE, TILE + width)
    low_rows, high_cols = slice(EDGE + p_rows, 2 * EDGE + p_rows), slice(TILE + width, 2 * TILE + width)
    pieces = [
        ((-1, 0), all_rows, left, inner_rows, slice(0, TILE)),
        ((1, 0), all_rows, right, inner_rows, high_cols),
        ((0, -1), top, all_cols, slice(0, EDGE), inner_cols),
        ((0, 1), bottom, all_cols, low_rows, inner_cols),
        ((-1, -1), top, left, slice(0, EDGE), slice(0, TILE)),
        ((1, -1), top, right, slice(0, EDGE), high_cols),
        ((-1, 1), bottom, left, low_rows, slice(0, TILE)),
        ((1, 1), bottom, right, low_rows, high_cols),
    ]
    halo_copies = []
    for n, ((s_ra, s_dec), my_rows, my_cols, rows, cols) in enumerate(pieces):
        copy = pltpu.make_async_remote_copy(
            src_ref=template_ref.at[my_rows, my_cols],
            dst_ref=ext_ref.at[rows, cols],
            send_sem=halo_send.at[n],
            recv_sem=halo_recv.at[n],
            device_id=peer(-s_ra, -s_dec),
            device_id_type=MESH,
        )
        copy.start()
        halo_copies.append(copy)
    sign = 2 * lax.rem(ra, 2) - 1

    def grid_copy(src, slot, d_ra):
        return pltpu.make_async_remote_copy(
            src_ref=src,
            dst_ref=arrived_ref.at[slot],
            send_sem=grid_send.at[slot],
            recv_sem=grid_recv.at[slot],
            device_id=peer(d_ra, 0),
            device_id_type=MESH,
        )

    to_partner = grid_copy(grid_ref.at[SPAN - sign], OWN, -sign)
    to_combine = grid_copy(grid_ref.at[SPAN - 2 * sign], MIXED, -sign)
    far = grid_copy(grid_ref.at[SPAN + 2 * sign], FAR, 2 * sign)
    near = grid_copy(combined_ref, NEAR, sign)
    for copy in (to_partner, to_combine, far):
        copy.start()

    level = level_ref[...]
    level_sq = level * level

    def weight_step(k, carry):
        vrow = jnp.broadcast_to(vtaps_ref[pl.ds(k, 1), :], (p_rows, BLOCK))
        shifted_taps = pltpu.roll(vrow, EDGE - HALF, 1, stride=1, stride_axis=0)
        plain = coef_ref[k, 0] + coef_ref[k, 1] * level + coef_ref[k, 2] * level_sq
        with_cos = coef_ref[k, 3] + coef_ref[k, 5] * level
        col = pl.multiple_of(k * BLOCK, BLOCK)
        for term, scale in enumerate((plain, with_cos, coef_ref[k, 4])):
            w = scale * shifted_taps
            high = w.astype(bf16)
            low = (w - high.astype(f32)).astype(bf16)
            weights_ref[term * p_rows:(term + 1) * p_rows, pl.ds(col, BLOCK)] = high
            weights_ref[(3 + term) * p_rows:(4 + term) * p_rows, pl.ds(col, BLOCK)] = low
        rp_ref[pl.ds(k * BLOCK + ROWS_PAD, BLOCK - ROWS_PAD), :] = jnp.zeros(
            (BLOCK - ROWS_PAD, rp_ref.shape[1]), bf16
        )
        return carry

    lax.fori_loop(0, n_basis, weight_step, 0)

    for copy in halo_copies:
        copy.wait()
    to_combine.wait_recv()
    combined_ref[...] = grid_ref[SPAN + sign] + arrived_ref[MIXED]
    near.start()
    keep_top = dec > 0
    keep_bottom = dec < n_dec - 1
    ext_ref[0:EDGE, :] = jnp.where(keep_top, ext_ref[0:EDGE, :], jnp.zeros_like(ext_ref[0:EDGE, :]))
    ext_ref[EDGE + p_rows:, :] = jnp.where(
        keep_bottom, ext_ref[EDGE + p_rows:, :], jnp.zeros_like(ext_ref[EDGE + p_rows:, :])
    )
    for t in range(n_tiles):
        slab = ext_ref[:, t * TILE:t * TILE + 3 * TILE].astype(f32)
        slab = pltpu.roll(slab, 3 * TILE - (TILE - HALF), 1)
        windows_ref[t * ROWS_PAD:(t + 1) * ROWS_PAD, :] = slab[:, 0:WIN].astype(bf16)

    def row_step(step, carry):
        bands = []
        for half in range(2):
            urow = jnp.broadcast_to(utaps_ref[pl.ds(2 * step + half, 1), :], (TILE, WIN))
            bands.append(pltpu.roll(urow, 0, 1, stride=1, stride_axis=0))
        band_t = jnp.concatenate(bands, axis=0).astype(bf16)
        part = lax.dot_general(
            windows_ref[...], band_t, (((1,), (1,)), ((), ())), preferred_element_type=f32
        ).astype(bf16)
        for half in range(2):
            base = pl.multiple_of((2 * step + half) * BLOCK, BLOCK)
            for t in range(n_tiles):
                rp_ref[pl.ds(base, ROWS_PAD), t * TILE:(t + 1) * TILE] = part[
                    t * ROWS_PAD:(t + 1) * ROWS_PAD, half * TILE:(half + 1) * TILE
                ]
        return carry

    lax.fori_loop(0, n_basis // 2, row_step, 0)

    chunk = 256

    def col_step(step, carry):
        col = pl.multiple_of(step * chunk, chunk)
        sums = jnp.dot(weights_ref[...], rp_ref[:, pl.ds(col, chunk)], preferred_element_type=f32)
        lo = 3 * p_rows
        plain = sums[0:p_rows] + sums[lo:lo + p_rows]
        with_cos = sums[p_rows:2 * p_rows] + sums[lo + p_rows:lo + 2 * p_rows]
        with_sin = sums[2 * p_rows:3 * p_rows] + sums[lo + 2 * p_rows:lo + 3 * p_rows]
        cosine = trig_ref[0:1, pl.ds(col, chunk)]
        sine = trig_ref[1:2, pl.ds(col, chunk)]
        out_ref[:, pl.ds(col, chunk)] = plain + cosine * with_cos + sine * with_sin
        return carry

    lax.fori_loop(0, out_ref.shape[1] // chunk, col_step, 0)

    to_partner.wait()
    to_combine.wait_send()
    far.wait()
    near.wait()
    science = grid_ref[SPAN] + arrived_ref[OWN] + arrived_ref[NEAR] + arrived_ref[FAR]
    out_ref[...] = science - out_ref[...]


def difference_image(template, grid, row_taps, col_taps, coef, level, trig):
    p_rows = level.shape[0]
    width = trig.shape[1]
    n_tiles = width // TILE
    k_count = row_taps.shape[0]
    n_basis = k_count + (k_count % 2)
    utaps = jnp.pad(row_taps.astype(jnp.float32), ((0, n_basis - k_count), (0, WIN - row_taps.shape[1])))
    vtaps = jnp.pad(col_taps.astype(jnp.float32), ((0, n_basis - k_count), (0, BLOCK - col_taps.shape[1])))
    coef = jnp.pad(coef, ((0, n_basis - k_count), (0, 0)))
    level = jnp.broadcast_to(level[:, None], (p_rows, BLOCK))
    flops = 2 * n_tiles * ROWS_PAD * WIN * n_basis * TILE + 2 * 6 * p_rows * n_basis * BLOCK * width
    vmem = pl.BlockSpec(memory_space=pltpu.VMEM)
    n_out = 2 * SPAN
    return pl.pallas_call(
        functools.partial(conv_kernel, n_tiles, n_basis, p_rows),
        out_shape=jax.ShapeDtypeStruct((p_rows, width), jnp.float32),
        in_specs=[pl.BlockSpec(memory_space=pltpu.SMEM)] + [vmem] * 6,
        out_specs=vmem,
        scratch_shapes=[
            pltpu.VMEM((n_basis * BLOCK, width), jnp.bfloat16),
            pltpu.VMEM((n_tiles * ROWS_PAD, WIN), jnp.bfloat16),
            pltpu.VMEM((6 * p_rows, n_basis * BLOCK), jnp.bfloat16),
            pltpu.VMEM((p_rows + 2 * EDGE, width + 2 * TILE), jnp.bfloat16),
            pltpu.VMEM((n_out, p_rows, width), jnp.float32),
            pltpu.VMEM((p_rows, width), jnp.float32),
            pltpu.SemaphoreType.DMA((8,)),
            pltpu.SemaphoreType.DMA((8,)),
            pltpu.SemaphoreType.DMA((n_out,)),
            pltpu.SemaphoreType.DMA((n_out,)),
        ],
        compiler_params=pltpu.CompilerParams(
            vmem_limit_bytes=60 * 1024 * 1024, collective_id=0, has_side_effects=True
        ),
        cost_estimate=pl.CostEstimate(flops=flops, transcendentals=0, bytes_accessed=8 * 1024 * 1024),
    )(coef, utaps, vtaps, level, trig, template, grid)


def local(exposure, slots, target_rows, template, row_taps, col_taps, coef):
    e_rows, width = exposure.shape
    p_rows = template.shape[0]
    n_slots = 2 * SPAN + 1
    slot_ids = slots[:, 0]
    flat_place = slot_ids * p_rows + target_rows
    select = (jnp.arange(n_slots * p_rows, dtype=jnp.int32)[:, None] == flat_place[None, :]).astype(jnp.float32)
    partial = jnp.dot(
        select, exposure, precision=lax.Precision.HIGHEST, preferred_element_type=jnp.float32
    ).reshape(n_slots, p_rows, width)
    total_rows = p_rows * lax.axis_size("dec")
    total_cols = width * lax.axis_size("ra")
    rows_y = lax.axis_index("dec") * p_rows + jnp.arange(p_rows, dtype=jnp.int32)
    level = (2 * rows_y + 1).astype(jnp.float32) / total_rows - 1.0
    cols_x = lax.axis_index("ra") * width + jnp.arange(width, dtype=jnp.int32)
    phase = (2 * cols_x + 1).astype(jnp.float32) * (math.pi / total_cols)
    trig = jnp.stack([jnp.cos(phase), jnp.sin(phase)])

    return difference_image(template, partial, row_taps, col_taps, coef, level, trig)


def solution(mesh):
    return jax.shard_map(
        local,
        mesh=mesh,
        in_specs=(
            P(("ra", "dec"), None),
            P(("ra", "dec"), None),
            P(("ra", "dec")),
            P("dec", "ra"),
            P(),
            P(),
            P(),
        ),
        out_specs=P("dec", "ra"),
        check_vma=False,
    )
```

```python
import functools
import math

import jax
import jax.numpy as jnp
from jax import lax
from jax.experimental import pallas as pl
from jax.experimental.pallas import tpu as pltpu
from jax.sharding import PartitionSpec as P

SPAN = 2
HALF = 10
TILE = 128
WIN = 256
ROWS_PAD = 96
BLOCK = 128
EDGE = 16
MESH = pl.DeviceIdType.MESH
OWN, MIXED, NEAR, FAR = range(4)


def build_weights(coef_ref, vtaps_ref, weights_ref, rp_ref, n_basis, p_rows):
    f32, bf16 = jnp.float32, jnp.bfloat16
    rows = lax.axis_index("dec") * p_rows + lax.broadcasted_iota(jnp.int32, (p_rows, BLOCK), 0)
    level = (2 * rows + 1).astype(f32) / (p_rows * lax.axis_size("dec")) - 1.0
    level_sq = level * level

    def weight_step(k, carry):
        vrow = jnp.broadcast_to(vtaps_ref[pl.ds(k, 1), :], (p_rows, BLOCK))
        shifted_taps = pltpu.roll(vrow, EDGE - HALF, 1, stride=1, stride_axis=0)
        plain = coef_ref[k, 0] + coef_ref[k, 1] * level + coef_ref[k, 2] * level_sq
        with_cos = coef_ref[k, 3] + coef_ref[k, 5] * level
        col = pl.multiple_of(k * BLOCK, BLOCK)
        for term, scale in enumerate((plain, with_cos, coef_ref[k, 4])):
            w = scale * shifted_taps
            high = w.astype(bf16)
            low = (w - high.astype(f32)).astype(bf16)
            weights_ref[term * p_rows:(term + 1) * p_rows, pl.ds(col, BLOCK)] = high
            weights_ref[(3 + term) * p_rows:(4 + term) * p_rows, pl.ds(col, BLOCK)] = low
        rp_ref[pl.ds(k * BLOCK + ROWS_PAD, BLOCK - ROWS_PAD), :] = jnp.zeros(
            (BLOCK - ROWS_PAD, rp_ref.shape[1]), bf16
        )
        return carry

    k_count = coef_ref.shape[0]
    lax.fori_loop(0, k_count, weight_step, 0)
    for k in range(k_count, n_basis):
        weights_ref[:, k * BLOCK:(k + 1) * BLOCK] = jnp.zeros((weights_ref.shape[0], BLOCK), bf16)
        rp_ref[k * BLOCK + ROWS_PAD:(k + 1) * BLOCK, :] = jnp.zeros((BLOCK - ROWS_PAD, rp_ref.shape[1]), bf16)


def conv_kernel(n_tiles, n_basis, p_rows, coef_ref, utaps_ref, vtaps_ref, template_ref,
                grid_ref, out_ref, rp_ref, windows_ref, weights_ref, ext_ref, arrived_ref, combined_ref,
                halo_send, halo_recv, grid_send, grid_recv):
    f32, bf16 = jnp.float32, jnp.bfloat16
    n_ra, n_dec = lax.axis_size("ra"), lax.axis_size("dec")
    ra, dec = lax.axis_index("ra"), lax.axis_index("dec")

    def peer(d_ra, d_dec):
        return (lax.rem(ra + d_ra + n_ra, n_ra), lax.rem(dec + d_dec + n_dec, n_dec))

    width = template_ref.shape[1]
    ext_ref[EDGE:EDGE + p_rows, TILE:TILE + width] = template_ref[...]
    partners = [(1, 0), (-1, 0), (2, 0), (-2, 0), (0, 1), (0, -1), (1, 1), (1, -1), (-1, 1), (-1, -1)]
    barrier = pltpu.get_barrier_semaphore()
    for d_ra, d_dec in partners:
        pl.semaphore_signal(barrier, inc=1, device_id=peer(d_ra, d_dec), device_id_type=MESH)

    build_weights(coef_ref, vtaps_ref, weights_ref, rp_ref, n_basis, p_rows)
    pl.semaphore_wait(barrier, len(partners))

    top, bottom = slice(p_rows - EDGE, p_rows), slice(0, EDGE)
    left, right = slice(width - TILE, width), slice(0, TILE)
    all_rows, all_cols = slice(0, p_rows), slice(0, width)
    inner_rows, inner_cols = slice(EDGE, EDGE + p_rows), slice(TILE, TILE + width)
    low_rows, high_cols = slice(EDGE + p_rows, 2 * EDGE + p_rows), slice(TILE + width, 2 * TILE + width)
    pieces = [
        ((-1, 0), all_rows, left, inner_rows, slice(0, TILE)),
        ((1, 0), all_rows, right, inner_rows, high_cols),
        ((0, -1), top, all_cols, slice(0, EDGE), inner_cols),
        ((0, 1), bottom, all_cols, low_rows, inner_cols),
        ((-1, -1), top, left, slice(0, EDGE), slice(0, TILE)),
        ((1, -1), top, right, slice(0, EDGE), high_cols),
        ((-1, 1), bottom, left, low_rows, slice(0, TILE)),
        ((1, 1), bottom, right, low_rows, high_cols),
    ]
    halo_copies = []
    for n, ((s_ra, s_dec), my_rows, my_cols, rows, cols) in enumerate(pieces):
        copy = pltpu.make_async_remote_copy(
            src_ref=template_ref.at[my_rows, my_cols],
            dst_ref=ext_ref.at[rows, cols],
            send_sem=halo_send.at[n],
            recv_sem=halo_recv.at[n],
            device_id=peer(-s_ra, -s_dec),
            device_id_type=MESH,
        )
        copy.start()
        halo_copies.append(copy)
    sign = 2 * lax.rem(ra, 2) - 1

    def grid_copy(src, slot, d_ra):
        return pltpu.make_async_remote_copy(
            src_ref=src,
            dst_ref=arrived_ref.at[slot],
            send_sem=grid_send.at[slot],
            recv_sem=grid_recv.at[slot],
            device_id=peer(d_ra, 0),
            device_id_type=MESH,
        )

    to_partner = grid_copy(grid_ref.at[SPAN - sign], OWN, -sign)
    to_combine = grid_copy(grid_ref.at[SPAN - 2 * sign], MIXED, -sign)
    far = grid_copy(grid_ref.at[SPAN + 2 * sign], FAR, 2 * sign)
    near = grid_copy(combined_ref, NEAR, sign)
    for copy in (to_partner, to_combine, far):
        copy.start()

    to_combine.wait_recv()
    combined_ref[...] = grid_ref[SPAN + sign] + arrived_ref[MIXED]
    near.start()
    for copy in halo_copies:
        copy.wait()
    keep_top = dec > 0
    keep_bottom = dec < n_dec - 1
    ext_ref[0:EDGE, :] = jnp.where(keep_top, ext_ref[0:EDGE, :], jnp.zeros_like(ext_ref[0:EDGE, :]))
    ext_ref[EDGE + p_rows:, :] = jnp.where(
        keep_bottom, ext_ref[EDGE + p_rows:, :], jnp.zeros_like(ext_ref[EDGE + p_rows:, :])
    )
    for t in range(n_tiles):
        slab = ext_ref[:, t * TILE:t * TILE + 3 * TILE].astype(f32)
        slab = pltpu.roll(slab, 3 * TILE - (TILE - HALF), 1)
        windows_ref[t * ROWS_PAD:(t + 1) * ROWS_PAD, :] = slab[:, 0:WIN].astype(bf16)

    def row_step(step, carry):
        bands = []
        for half in range(2):
            urow = jnp.broadcast_to(utaps_ref[pl.ds(2 * step + half, 1), :], (TILE, WIN))
            bands.append(pltpu.roll(urow, 0, 1, stride=1, stride_axis=0))
        band_t = jnp.concatenate(bands, axis=0).astype(bf16)
        part = lax.dot_general(
            windows_ref[...], band_t, (((1,), (1,)), ((), ())), preferred_element_type=f32
        ).astype(bf16)
        for half in range(2):
            base = pl.multiple_of((2 * step + half) * BLOCK, BLOCK)
            for t in range(n_tiles):
                rp_ref[pl.ds(base, ROWS_PAD), t * TILE:(t + 1) * TILE] = part[
                    t * ROWS_PAD:(t + 1) * ROWS_PAD, half * TILE:(half + 1) * TILE
                ]
        return carry

    lax.fori_loop(0, n_basis // 2, row_step, 0)

    chunk = 256

    def col_step(step, carry):
        col = pl.multiple_of(step * chunk, chunk)
        sums = jnp.dot(weights_ref[...], rp_ref[:, pl.ds(col, chunk)], preferred_element_type=f32)
        lo = 3 * p_rows
        plain = sums[0:p_rows] + sums[lo:lo + p_rows]
        with_cos = sums[p_rows:2 * p_rows] + sums[lo + p_rows:lo + 2 * p_rows]
        with_sin = sums[2 * p_rows:3 * p_rows] + sums[lo + 2 * p_rows:lo + 3 * p_rows]
        cols = ra * width + col + lax.broadcasted_iota(jnp.int32, (1, chunk), 1)
        phase = (2 * cols + 1).astype(f32) * (math.pi / (width * n_ra))
        cosine = jnp.cos(phase)
        sine = jnp.sin(phase)
        out_ref[:, pl.ds(col, chunk)] = plain + cosine * with_cos + sine * with_sin
        return carry

    lax.fori_loop(0, out_ref.shape[1] // chunk, col_step, 0)

    to_partner.wait()
    to_combine.wait_send()
    far.wait()
    near.wait()
    science = grid_ref[SPAN] + arrived_ref[OWN] + arrived_ref[NEAR] + arrived_ref[FAR]
    out_ref[...] = science - out_ref[...]


def difference_image(template, grid, row_taps, col_taps, coef):
    p_rows, width = template.shape
    n_tiles = width // TILE
    k_count = row_taps.shape[0]
    n_basis = k_count + (k_count % 2)
    utaps = jnp.pad(row_taps.astype(jnp.float32), ((0, n_basis - k_count), (0, WIN - row_taps.shape[1])))
    vtaps = jnp.pad(col_taps.astype(jnp.float32), ((0, n_basis - k_count), (0, BLOCK - col_taps.shape[1])))
    flops = 2 * n_tiles * ROWS_PAD * WIN * n_basis * TILE + 2 * 6 * p_rows * n_basis * BLOCK * width
    vmem = pl.BlockSpec(memory_space=pltpu.VMEM)
    n_out = 2 * SPAN
    return pl.pallas_call(
        functools.partial(conv_kernel, n_tiles, n_basis, p_rows),
        out_shape=jax.ShapeDtypeStruct((p_rows, width), jnp.float32),
        in_specs=[pl.BlockSpec(memory_space=pltpu.SMEM)] + [vmem] * 4,
        out_specs=vmem,
        scratch_shapes=[
            pltpu.VMEM((n_basis * BLOCK, width), jnp.bfloat16),
            pltpu.VMEM((n_tiles * ROWS_PAD, WIN), jnp.bfloat16),
            pltpu.VMEM((6 * p_rows, n_basis * BLOCK), jnp.bfloat16),
            pltpu.VMEM((p_rows + 2 * EDGE, width + 2 * TILE), jnp.bfloat16),
            pltpu.VMEM((n_out, p_rows, width), jnp.float32),
            pltpu.VMEM((p_rows, width), jnp.float32),
            pltpu.SemaphoreType.DMA((8,)),
            pltpu.SemaphoreType.DMA((8,)),
            pltpu.SemaphoreType.DMA((n_out,)),
            pltpu.SemaphoreType.DMA((n_out,)),
        ],
        compiler_params=pltpu.CompilerParams(
            vmem_limit_bytes=60 * 1024 * 1024, collective_id=0, has_side_effects=True
        ),
        cost_estimate=pl.CostEstimate(flops=flops, transcendentals=0, bytes_accessed=8 * 1024 * 1024),
    )(coef, utaps, vtaps, template, grid)


def local(exposure, slots, target_rows, template, row_taps, col_taps, coef):
    e_rows, width = exposure.shape
    p_rows = template.shape[0]
    n_slots = 2 * SPAN + 1
    place = jnp.arange(n_slots * p_rows, dtype=jnp.int32)
    select = (
        (place[:, None] // p_rows == slots[None, :, 0]) & (place[:, None] % p_rows == target_rows[None, :])
    ).astype(jnp.float32)
    partial = jnp.dot(
        select, exposure, precision=lax.Precision.HIGHEST, preferred_element_type=jnp.float32
    ).reshape(n_slots, p_rows, width)
    return difference_image(template, partial, row_taps, col_taps, coef)


def solution(mesh):
    return jax.shard_map(
        local,
        mesh=mesh,
        in_specs=(
            P(("ra", "dec"), None),
            P(("ra", "dec"), None),
            P(("ra", "dec")),
            P("dec", "ra"),
            P(),
            P(),
            P(),
        ),
        out_specs=P("dec", "ra"),
        check_vma=False,
    )
```

```python
import functools
import math

import jax
import jax.numpy as jnp
from jax import lax
from jax.experimental import pallas as pl
from jax.experimental.pallas import tpu as pltpu
from jax.sharding import PartitionSpec as P

SPAN = 2
HALF = 10
TILE = 128
WIN = 256
ROWS_PAD = 96
BLOCK = 128
EDGE = 16
MESH = pl.DeviceIdType.MESH
OWN, MIXED, NEAR, FAR = range(4)


def build_weights(coef_ref, vtaps_ref, weights_ref, rp_ref, n_basis, p_rows):
    f32, bf16 = jnp.float32, jnp.bfloat16
    rows = lax.axis_index("dec") * p_rows + lax.broadcasted_iota(jnp.int32, (p_rows, BLOCK), 0)
    level = (2 * rows + 1).astype(f32) / (p_rows * lax.axis_size("dec")) - 1.0
    level_sq = level * level

    def weight_step(k, carry):
        vrow = jnp.broadcast_to(vtaps_ref[pl.ds(k, 1), :], (p_rows, BLOCK))
        shifted_taps = pltpu.roll(vrow, EDGE - HALF, 1, stride=1, stride_axis=0)
        plain = coef_ref[k, 0] + coef_ref[k, 1] * level + coef_ref[k, 2] * level_sq
        with_cos = coef_ref[k, 3] + coef_ref[k, 5] * level
        col = pl.multiple_of(k * BLOCK, BLOCK)
        for term, scale in enumerate((plain, with_cos, coef_ref[k, 4])):
            w = scale * shifted_taps
            high = w.astype(bf16)
            low = (w - high.astype(f32)).astype(bf16)
            weights_ref[term * p_rows:(term + 1) * p_rows, pl.ds(col, BLOCK)] = high
            weights_ref[(3 + term) * p_rows:(4 + term) * p_rows, pl.ds(col, BLOCK)] = low
        rp_ref[pl.ds(k * BLOCK + ROWS_PAD, BLOCK - ROWS_PAD), :] = jnp.zeros(
            (BLOCK - ROWS_PAD, rp_ref.shape[1]), bf16
        )
        return carry

    k_count = coef_ref.shape[0]
    lax.fori_loop(0, k_count, weight_step, 0)
    for k in range(k_count, n_basis):
        weights_ref[:, k * BLOCK:(k + 1) * BLOCK] = jnp.zeros((weights_ref.shape[0], BLOCK), bf16)
        rp_ref[k * BLOCK + ROWS_PAD:(k + 1) * BLOCK, :] = jnp.zeros((BLOCK - ROWS_PAD, rp_ref.shape[1]), bf16)


def conv_kernel(n_tiles, n_basis, p_rows, coef_ref, utaps_ref, vtaps_ref, template_ref,
                grid_ref, out_ref, rp_ref, windows_ref, weights_ref, ext_ref, arrived_ref, combined_ref,
                halo_send, halo_recv, grid_send, grid_recv):
    f32, bf16 = jnp.float32, jnp.bfloat16
    n_ra, n_dec = lax.axis_size("ra"), lax.axis_size("dec")
    ra, dec = lax.axis_index("ra"), lax.axis_index("dec")

    def peer(d_ra, d_dec):
        return (lax.rem(ra + d_ra + n_ra, n_ra), lax.rem(dec + d_dec + n_dec, n_dec))

    width = template_ref.shape[1]
    ext_ref[EDGE:EDGE + p_rows, TILE:TILE + width] = template_ref[...]
    partners = [(1, 0), (-1, 0), (2, 0), (-2, 0), (0, 1), (0, -1), (1, 1), (1, -1), (-1, 1), (-1, -1)]
    barrier = pltpu.get_barrier_semaphore()
    for d_ra, d_dec in partners:
        pl.semaphore_signal(barrier, inc=1, device_id=peer(d_ra, d_dec), device_id_type=MESH)

    build_weights(coef_ref, vtaps_ref, weights_ref, rp_ref, n_basis, p_rows)
    pl.semaphore_wait(barrier, len(partners))

    top, bottom = slice(p_rows - EDGE, p_rows), slice(0, EDGE)
    left, right = slice(width - TILE, width), slice(0, TILE)
    all_rows, all_cols = slice(0, p_rows), slice(0, width)
    inner_rows, inner_cols = slice(EDGE, EDGE + p_rows), slice(TILE, TILE + width)
    low_rows, high_cols = slice(EDGE + p_rows, 2 * EDGE + p_rows), slice(TILE + width, 2 * TILE + width)
    pieces = [
        ((-1, 0), all_rows, left, inner_rows, slice(0, TILE)),
        ((1, 0), all_rows, right, inner_rows, high_cols),
        ((0, -1), top, all_cols, slice(0, EDGE), inner_cols),
        ((0, 1), bottom, all_cols, low_rows, inner_cols),
        ((-1, -1), top, left, slice(0, EDGE), slice(0, TILE)),
        ((1, -1), top, right, slice(0, EDGE), high_cols),
        ((-1, 1), bottom, left, low_rows, slice(0, TILE)),
        ((1, 1), bottom, right, low_rows, high_cols),
    ]
    sign = 2 * lax.rem(ra, 2) - 1

    def grid_copy(src, slot, d_ra):
        return pltpu.make_async_remote_copy(
            src_ref=src,
            dst_ref=arrived_ref.at[slot],
            send_sem=grid_send.at[slot],
            recv_sem=grid_recv.at[slot],
            device_id=peer(d_ra, 0),
            device_id_type=MESH,
        )

    to_partner = grid_copy(grid_ref.at[SPAN - sign], OWN, -sign)
    to_combine = grid_copy(grid_ref.at[SPAN - 2 * sign], MIXED, -sign)
    far = grid_copy(grid_ref.at[SPAN + 2 * sign], FAR, 2 * sign)
    near = grid_copy(combined_ref, NEAR, sign)
    for copy in (to_partner, to_combine, far):
        copy.start()

    halo_copies = []
    for n, ((s_ra, s_dec), my_rows, my_cols, rows, cols) in enumerate(pieces):
        copy = pltpu.make_async_remote_copy(
            src_ref=template_ref.at[my_rows, my_cols],
            dst_ref=ext_ref.at[rows, cols],
            send_sem=halo_send.at[n],
            recv_sem=halo_recv.at[n],
            device_id=peer(-s_ra, -s_dec),
            device_id_type=MESH,
        )
        copy.start()
        halo_copies.append(copy)

    to_combine.wait_recv()
    combined_ref[...] = grid_ref[SPAN + sign] + arrived_ref[MIXED]
    near.start()
    for copy in halo_copies:
        copy.wait()
    keep_top = dec > 0
    keep_bottom = dec < n_dec - 1
    ext_ref[0:EDGE, :] = jnp.where(keep_top, ext_ref[0:EDGE, :], jnp.zeros_like(ext_ref[0:EDGE, :]))
    ext_ref[EDGE + p_rows:, :] = jnp.where(
        keep_bottom, ext_ref[EDGE + p_rows:, :], jnp.zeros_like(ext_ref[EDGE + p_rows:, :])
    )
    for t in range(n_tiles):
        slab = ext_ref[:, t * TILE:t * TILE + 3 * TILE].astype(f32)
        slab = pltpu.roll(slab, 3 * TILE - (TILE - HALF), 1)
        windows_ref[t * ROWS_PAD:(t + 1) * ROWS_PAD, :] = slab[:, 0:WIN].astype(bf16)

    def row_step(step, carry):
        bands = []
        for half in range(2):
            urow = jnp.broadcast_to(utaps_ref[pl.ds(2 * step + half, 1), :], (TILE, WIN))
            bands.append(pltpu.roll(urow, 0, 1, stride=1, stride_axis=0))
        band_t = jnp.concatenate(bands, axis=0).astype(bf16)
        part = lax.dot_general(
            windows_ref[...], band_t, (((1,), (1,)), ((), ())), preferred_element_type=f32
        ).astype(bf16)
        for half in range(2):
            base = pl.multiple_of((2 * step + half) * BLOCK, BLOCK)
            for t in range(n_tiles):
                rp_ref[pl.ds(base, ROWS_PAD), t * TILE:(t + 1) * TILE] = part[
                    t * ROWS_PAD:(t + 1) * ROWS_PAD, half * TILE:(half + 1) * TILE
                ]
        return carry

    lax.fori_loop(0, n_basis // 2, row_step, 0)

    chunk = 256

    def col_step(step, carry):
        col = pl.multiple_of(step * chunk, chunk)
        sums = jnp.dot(weights_ref[...], rp_ref[:, pl.ds(col, chunk)], preferred_element_type=f32)
        lo = 3 * p_rows
        plain = sums[0:p_rows] + sums[lo:lo + p_rows]
        with_cos = sums[p_rows:2 * p_rows] + sums[lo + p_rows:lo + 2 * p_rows]
        with_sin = sums[2 * p_rows:3 * p_rows] + sums[lo + 2 * p_rows:lo + 3 * p_rows]
        cols = ra * width + col + lax.broadcasted_iota(jnp.int32, (1, chunk), 1)
        phase = (2 * cols + 1).astype(f32) * (math.pi / (width * n_ra))
        cosine = jnp.cos(phase)
        sine = jnp.sin(phase)
        out_ref[:, pl.ds(col, chunk)] = plain + cosine * with_cos + sine * with_sin
        return carry

    lax.fori_loop(0, out_ref.shape[1] // chunk, col_step, 0)

    to_partner.wait()
    to_combine.wait_send()
    far.wait()
    near.wait()
    science = grid_ref[SPAN] + arrived_ref[OWN] + arrived_ref[NEAR] + arrived_ref[FAR]
    out_ref[...] = science - out_ref[...]


def difference_image(template, grid, row_taps, col_taps, coef):
    p_rows, width = template.shape
    n_tiles = width // TILE
    k_count = row_taps.shape[0]
    n_basis = k_count + (k_count % 2)
    utaps = jnp.pad(row_taps.astype(jnp.float32), ((0, n_basis - k_count), (0, WIN - row_taps.shape[1])))
    vtaps = jnp.pad(col_taps.astype(jnp.float32), ((0, n_basis - k_count), (0, BLOCK - col_taps.shape[1])))
    flops = 2 * n_tiles * ROWS_PAD * WIN * n_basis * TILE + 2 * 6 * p_rows * n_basis * BLOCK * width
    vmem = pl.BlockSpec(memory_space=pltpu.VMEM)
    n_out = 2 * SPAN
    return pl.pallas_call(
        functools.partial(conv_kernel, n_tiles, n_basis, p_rows),
        out_shape=jax.ShapeDtypeStruct((p_rows, width), jnp.float32),
        in_specs=[pl.BlockSpec(memory_space=pltpu.SMEM)] + [vmem] * 4,
        out_specs=vmem,
        scratch_shapes=[
            pltpu.VMEM((n_basis * BLOCK, width), jnp.bfloat16),
            pltpu.VMEM((n_tiles * ROWS_PAD, WIN), jnp.bfloat16),
            pltpu.VMEM((6 * p_rows, n_basis * BLOCK), jnp.bfloat16),
            pltpu.VMEM((p_rows + 2 * EDGE, width + 2 * TILE), jnp.bfloat16),
            pltpu.VMEM((n_out, p_rows, width), jnp.float32),
            pltpu.VMEM((p_rows, width), jnp.float32),
            pltpu.SemaphoreType.DMA((8,)),
            pltpu.SemaphoreType.DMA((8,)),
            pltpu.SemaphoreType.DMA((n_out,)),
            pltpu.SemaphoreType.DMA((n_out,)),
        ],
        compiler_params=pltpu.CompilerParams(
            vmem_limit_bytes=60 * 1024 * 1024, collective_id=0, has_side_effects=True
        ),
        cost_estimate=pl.CostEstimate(flops=flops, transcendentals=0, bytes_accessed=8 * 1024 * 1024),
    )(coef, utaps, vtaps, template, grid)


def local(exposure, slots, target_rows, template, row_taps, col_taps, coef):
    e_rows, width = exposure.shape
    p_rows = template.shape[0]
    n_slots = 2 * SPAN + 1
    place = jnp.arange(n_slots * p_rows, dtype=jnp.int32)
    select = (
        (place[:, None] // p_rows == slots[None, :, 0]) & (place[:, None] % p_rows == target_rows[None, :])
    ).astype(jnp.float32)
    partial = jnp.dot(
        select, exposure, precision=lax.Precision.HIGHEST, preferred_element_type=jnp.float32
    ).reshape(n_slots, p_rows, width)
    return difference_image(template, partial, row_taps, col_taps, coef)


def solution(mesh):
    return jax.shard_map(
        local,
        mesh=mesh,
        in_specs=(
            P(("ra", "dec"), None),
            P(("ra", "dec"), None),
            P(("ra", "dec")),
            P("dec", "ra"),
            P(),
            P(),
            P(),
        ),
        out_specs=P("dec", "ra"),
        check_vma=False,
    )
```

```python
import functools
import math

import jax
import jax.numpy as jnp
from jax import lax
from jax.experimental import pallas as pl
from jax.experimental.pallas import tpu as pltpu
from jax.sharding import PartitionSpec as P

SPAN = 2
HALF = 10
TILE = 128
WIN = 256
ROWS_PAD = 96
BLOCK = 128
EDGE = 16
MESH = pl.DeviceIdType.MESH
OWN, MIXED, NEAR, FAR = range(4)


def build_weights(coef_ref, vtaps_ref, weights_ref, rp_ref, n_basis, p_rows):
    f32, bf16 = jnp.float32, jnp.bfloat16
    rows = lax.axis_index("dec") * p_rows + lax.broadcasted_iota(jnp.int32, (p_rows, BLOCK), 0)
    level = (2 * rows + 1).astype(f32) / (p_rows * lax.axis_size("dec")) - 1.0
    level_sq = level * level

    def weight_step(k, carry):
        vrow = jnp.broadcast_to(vtaps_ref[pl.ds(k, 1), :], (p_rows, BLOCK))
        shifted_taps = pltpu.roll(vrow, EDGE - HALF, 1, stride=1, stride_axis=0)
        plain = coef_ref[k, 0] + coef_ref[k, 1] * level + coef_ref[k, 2] * level_sq
        with_cos = coef_ref[k, 3] + coef_ref[k, 5] * level
        col = pl.multiple_of(k * BLOCK, BLOCK)
        for term, scale in enumerate((plain, with_cos, coef_ref[k, 4])):
            w = scale * shifted_taps
            high = w.astype(bf16)
            low = (w - high.astype(f32)).astype(bf16)
            weights_ref[term * p_rows:(term + 1) * p_rows, pl.ds(col, BLOCK)] = high
            weights_ref[(3 + term) * p_rows:(4 + term) * p_rows, pl.ds(col, BLOCK)] = low
        rp_ref[pl.ds(k * BLOCK + ROWS_PAD, BLOCK - ROWS_PAD), :] = jnp.zeros(
            (BLOCK - ROWS_PAD, rp_ref.shape[1]), bf16
        )
        return carry

    k_count = coef_ref.shape[0]
    lax.fori_loop(0, k_count, weight_step, 0)
    for k in range(k_count, n_basis):
        weights_ref[:, k * BLOCK:(k + 1) * BLOCK] = jnp.zeros((weights_ref.shape[0], BLOCK), bf16)
        rp_ref[k * BLOCK + ROWS_PAD:(k + 1) * BLOCK, :] = jnp.zeros((BLOCK - ROWS_PAD, rp_ref.shape[1]), bf16)


def conv_kernel(n_tiles, n_basis, p_rows, coef_ref, utaps_ref, vtaps_ref, template_ref,
                grid_ref, out_ref, rp_ref, windows_ref, weights_ref, ext_ref, arrived_ref, combined_ref,
                halo_send, halo_recv, grid_send, grid_recv):
    f32, bf16 = jnp.float32, jnp.bfloat16
    n_ra, n_dec = lax.axis_size("ra"), lax.axis_size("dec")
    ra, dec = lax.axis_index("ra"), lax.axis_index("dec")

    def peer(d_ra, d_dec):
        return (lax.rem(ra + d_ra + n_ra, n_ra), lax.rem(dec + d_dec + n_dec, n_dec))

    width = template_ref.shape[1]
    ext_ref[EDGE:EDGE + p_rows, TILE:TILE + width] = template_ref[...]
    partners = [(1, 0), (-1, 0), (2, 0), (-2, 0), (0, 1), (0, -1), (1, 1), (1, -1), (-1, 1), (-1, -1)]
    barrier = pltpu.get_barrier_semaphore()
    for d_ra, d_dec in partners:
        pl.semaphore_signal(barrier, inc=1, device_id=peer(d_ra, d_dec), device_id_type=MESH)

    build_weights(coef_ref, vtaps_ref, weights_ref, rp_ref, n_basis, p_rows)
    pl.semaphore_wait(barrier, len(partners))

    top, bottom = slice(p_rows - EDGE, p_rows), slice(0, EDGE)
    left, right = slice(width - TILE, width), slice(0, TILE)
    all_rows, all_cols = slice(0, p_rows), slice(0, width)
    inner_rows, inner_cols = slice(EDGE, EDGE + p_rows), slice(TILE, TILE + width)
    low_rows, high_cols = slice(EDGE + p_rows, 2 * EDGE + p_rows), slice(TILE + width, 2 * TILE + width)
    pieces = [
        ((-1, 0), all_rows, left, inner_rows, slice(0, TILE)),
        ((1, 0), all_rows, right, inner_rows, high_cols),
        ((0, -1), top, all_cols, slice(0, EDGE), inner_cols),
        ((0, 1), bottom, all_cols, low_rows, inner_cols),
        ((-1, -1), top, left, slice(0, EDGE), slice(0, TILE)),
        ((1, -1), top, right, slice(0, EDGE), high_cols),
        ((-1, 1), bottom, left, low_rows, slice(0, TILE)),
        ((1, 1), bottom, right, low_rows, high_cols),
    ]
    halo_copies = []
    for n, ((s_ra, s_dec), my_rows, my_cols, rows, cols) in enumerate(pieces):
        copy = pltpu.make_async_remote_copy(
            src_ref=template_ref.at[my_rows, my_cols],
            dst_ref=ext_ref.at[rows, cols],
            send_sem=halo_send.at[n],
            recv_sem=halo_recv.at[n],
            device_id=peer(-s_ra, -s_dec),
            device_id_type=MESH,
        )
        copy.start()
        halo_copies.append(copy)
    sign = 2 * lax.rem(ra, 2) - 1

    half = p_rows // 2

    class GridCopy:
        def __init__(self, src, slot, d_ra):
            self.parts = [
                pltpu.make_async_remote_copy(
                    src_ref=src.at[h * half:(h + 1) * half],
                    dst_ref=arrived_ref.at[slot, h * half:(h + 1) * half],
                    send_sem=grid_send.at[2 * slot + h],
                    recv_sem=grid_recv.at[2 * slot + h],
                    device_id=peer(d_ra, 0),
                    device_id_type=MESH,
                )
                for h in range(2)
            ]

        def start(self):
            for part in self.parts:
                part.start()

        def wait(self):
            for part in self.parts:
                part.wait()

        def wait_recv(self):
            for part in self.parts:
                part.wait_recv()

        def wait_send(self):
            for part in self.parts:
                part.wait_send()

    to_partner = GridCopy(grid_ref.at[SPAN - sign], OWN, -sign)
    to_combine = GridCopy(grid_ref.at[SPAN - 2 * sign], MIXED, -sign)
    far = GridCopy(grid_ref.at[SPAN + 2 * sign], FAR, 2 * sign)
    near = GridCopy(combined_ref, NEAR, sign)
    for copy in (to_partner, to_combine, far):
        copy.start()

    to_combine.wait_recv()
    combined_ref[...] = grid_ref[SPAN + sign] + arrived_ref[MIXED]
    near.start()
    for copy in halo_copies:
        copy.wait()
    keep_top = dec > 0
    keep_bottom = dec < n_dec - 1
    ext_ref[0:EDGE, :] = jnp.where(keep_top, ext_ref[0:EDGE, :], jnp.zeros_like(ext_ref[0:EDGE, :]))
    ext_ref[EDGE + p_rows:, :] = jnp.where(
        keep_bottom, ext_ref[EDGE + p_rows:, :], jnp.zeros_like(ext_ref[EDGE + p_rows:, :])
    )
    for t in range(n_tiles):
        slab = ext_ref[:, t * TILE:t * TILE + 3 * TILE].astype(f32)
        slab = pltpu.roll(slab, 3 * TILE - (TILE - HALF), 1)
        windows_ref[t * ROWS_PAD:(t + 1) * ROWS_PAD, :] = slab[:, 0:WIN].astype(bf16)

    def row_step(step, carry):
        bands = []
        for half in range(2):
            urow = jnp.broadcast_to(utaps_ref[pl.ds(2 * step + half, 1), :], (TILE, WIN))
            bands.append(pltpu.roll(urow, 0, 1, stride=1, stride_axis=0))
        band_t = jnp.concatenate(bands, axis=0).astype(bf16)
        part = lax.dot_general(
            windows_ref[...], band_t, (((1,), (1,)), ((), ())), preferred_element_type=f32
        ).astype(bf16)
        for half in range(2):
            base = pl.multiple_of((2 * step + half) * BLOCK, BLOCK)
            for t in range(n_tiles):
                rp_ref[pl.ds(base, ROWS_PAD), t * TILE:(t + 1) * TILE] = part[
                    t * ROWS_PAD:(t + 1) * ROWS_PAD, half * TILE:(half + 1) * TILE
                ]
        return carry

    lax.fori_loop(0, n_basis // 2, row_step, 0)

    chunk = 256

    def col_step(step, carry):
        col = pl.multiple_of(step * chunk, chunk)
        sums = jnp.dot(weights_ref[...], rp_ref[:, pl.ds(col, chunk)], preferred_element_type=f32)
        lo = 3 * p_rows
        plain = sums[0:p_rows] + sums[lo:lo + p_rows]
        with_cos = sums[p_rows:2 * p_rows] + sums[lo + p_rows:lo + 2 * p_rows]
        with_sin = sums[2 * p_rows:3 * p_rows] + sums[lo + 2 * p_rows:lo + 3 * p_rows]
        cols = ra * width + col + lax.broadcasted_iota(jnp.int32, (1, chunk), 1)
        phase = (2 * cols + 1).astype(f32) * (math.pi / (width * n_ra))
        cosine = jnp.cos(phase)
        sine = jnp.sin(phase)
        out_ref[:, pl.ds(col, chunk)] = plain + cosine * with_cos + sine * with_sin
        return carry

    lax.fori_loop(0, out_ref.shape[1] // chunk, col_step, 0)

    to_partner.wait()
    to_combine.wait_send()
    far.wait()
    near.wait()
    science = grid_ref[SPAN] + arrived_ref[OWN] + arrived_ref[NEAR] + arrived_ref[FAR]
    out_ref[...] = science - out_ref[...]


def difference_image(template, grid, row_taps, col_taps, coef):
    p_rows, width = template.shape
    n_tiles = width // TILE
    k_count = row_taps.shape[0]
    n_basis = k_count + (k_count % 2)
    utaps = jnp.pad(row_taps.astype(jnp.float32), ((0, n_basis - k_count), (0, WIN - row_taps.shape[1])))
    vtaps = jnp.pad(col_taps.astype(jnp.float32), ((0, n_basis - k_count), (0, BLOCK - col_taps.shape[1])))
    flops = 2 * n_tiles * ROWS_PAD * WIN * n_basis * TILE + 2 * 6 * p_rows * n_basis * BLOCK * width
    vmem = pl.BlockSpec(memory_space=pltpu.VMEM)
    n_out = 2 * SPAN
    return pl.pallas_call(
        functools.partial(conv_kernel, n_tiles, n_basis, p_rows),
        out_shape=jax.ShapeDtypeStruct((p_rows, width), jnp.float32),
        in_specs=[pl.BlockSpec(memory_space=pltpu.SMEM)] + [vmem] * 4,
        out_specs=vmem,
        scratch_shapes=[
            pltpu.VMEM((n_basis * BLOCK, width), jnp.bfloat16),
            pltpu.VMEM((n_tiles * ROWS_PAD, WIN), jnp.bfloat16),
            pltpu.VMEM((6 * p_rows, n_basis * BLOCK), jnp.bfloat16),
            pltpu.VMEM((p_rows + 2 * EDGE, width + 2 * TILE), jnp.bfloat16),
            pltpu.VMEM((n_out, p_rows, width), jnp.float32),
            pltpu.VMEM((p_rows, width), jnp.float32),
            pltpu.SemaphoreType.DMA((8,)),
            pltpu.SemaphoreType.DMA((8,)),
            pltpu.SemaphoreType.DMA((2 * n_out,)),
            pltpu.SemaphoreType.DMA((2 * n_out,)),
        ],
        compiler_params=pltpu.CompilerParams(
            vmem_limit_bytes=60 * 1024 * 1024, collective_id=0, has_side_effects=True
        ),
        cost_estimate=pl.CostEstimate(flops=flops, transcendentals=0, bytes_accessed=8 * 1024 * 1024),
    )(coef, utaps, vtaps, template, grid)


def local(exposure, slots, target_rows, template, row_taps, col_taps, coef):
    e_rows, width = exposure.shape
    p_rows = template.shape[0]
    n_slots = 2 * SPAN + 1
    place = jnp.arange(n_slots * p_rows, dtype=jnp.int32)
    select = (
        (place[:, None] // p_rows == slots[None, :, 0]) & (place[:, None] % p_rows == target_rows[None, :])
    ).astype(jnp.float32)
    partial = jnp.dot(
        select, exposure, precision=lax.Precision.HIGHEST, preferred_element_type=jnp.float32
    ).reshape(n_slots, p_rows, width)
    return difference_image(template, partial, row_taps, col_taps, coef)


def solution(mesh):
    return jax.shard_map(
        local,
        mesh=mesh,
        in_specs=(
            P(("ra", "dec"), None),
            P(("ra", "dec"), None),
            P(("ra", "dec")),
            P("dec", "ra"),
            P(),
            P(),
            P(),
        ),
        out_specs=P("dec", "ra"),
        check_vma=False,
    )
```

```python
import functools
import math

import jax
import jax.numpy as jnp
from jax import lax
from jax.experimental import pallas as pl
from jax.experimental.pallas import tpu as pltpu
from jax.sharding import PartitionSpec as P

SPAN = 2
HALF = 10
TILE = 128
WIN = 256
ROWS_PAD = 96
BLOCK = 128
EDGE = 16
MESH = pl.DeviceIdType.MESH
OWN, MIXED, NEAR, FAR = range(4)


def build_weights(coef_ref, vtaps_ref, weights_ref, rp_ref, n_basis, p_rows):
    f32, bf16 = jnp.float32, jnp.bfloat16
    rows = lax.axis_index("dec") * p_rows + lax.broadcasted_iota(jnp.int32, (p_rows, BLOCK), 0)
    level = (2 * rows + 1).astype(f32) / (p_rows * lax.axis_size("dec")) - 1.0
    level_sq = level * level

    def weight_step(k, carry):
        vrow = jnp.broadcast_to(vtaps_ref[pl.ds(k, 1), :], (p_rows, BLOCK))
        shifted_taps = pltpu.roll(vrow, EDGE - HALF, 1, stride=1, stride_axis=0)
        plain = coef_ref[k, 0] + coef_ref[k, 1] * level + coef_ref[k, 2] * level_sq
        with_cos = coef_ref[k, 3] + coef_ref[k, 5] * level
        col = pl.multiple_of(k * BLOCK, BLOCK)
        for term, scale in enumerate((plain, with_cos, coef_ref[k, 4])):
            w = scale * shifted_taps
            high = w.astype(bf16)
            low = (w - high.astype(f32)).astype(bf16)
            weights_ref[term * p_rows:(term + 1) * p_rows, pl.ds(col, BLOCK)] = high
            weights_ref[(3 + term) * p_rows:(4 + term) * p_rows, pl.ds(col, BLOCK)] = low
        rp_ref[pl.ds(k * BLOCK + ROWS_PAD, BLOCK - ROWS_PAD), :] = jnp.zeros(
            (BLOCK - ROWS_PAD, rp_ref.shape[1]), bf16
        )
        return carry

    k_count = coef_ref.shape[0]
    lax.fori_loop(0, k_count, weight_step, 0)
    for k in range(k_count, n_basis):
        weights_ref[:, k * BLOCK:(k + 1) * BLOCK] = jnp.zeros((weights_ref.shape[0], BLOCK), bf16)
        rp_ref[k * BLOCK + ROWS_PAD:(k + 1) * BLOCK, :] = jnp.zeros((BLOCK - ROWS_PAD, rp_ref.shape[1]), bf16)


def presum_rows(exposure_ref, slot_ref, target_ref, grid_ref, p_rows):
    f32, bf16 = jnp.float32, jnp.bfloat16
    n_slots, e_rows = grid_ref.shape[0], exposure_ref.shape[0]
    place = lax.broadcasted_iota(jnp.int32, (n_slots * p_rows, e_rows), 0)
    select = ((place // p_rows == slot_ref[...]) & (place % p_rows == target_ref[...])).astype(bf16)
    chunk = 512
    for c in range(exposure_ref.shape[1] // chunk):
        rows = exposure_ref[:, c * chunk:(c + 1) * chunk]
        first = rows.astype(bf16)
        rest = rows - first.astype(f32)
        second = rest.astype(bf16)
        third = (rest - second.astype(f32)).astype(bf16)
        total = jnp.dot(select, first, preferred_element_type=f32)
        total = total + jnp.dot(select, second, preferred_element_type=f32)
        total = total + jnp.dot(select, third, preferred_element_type=f32)
        for slot in range(n_slots):
            grid_ref[slot, :, c * chunk:(c + 1) * chunk] = total[slot * p_rows:(slot + 1) * p_rows]


def conv_kernel(n_tiles, n_basis, p_rows, coef_ref, utaps_ref, vtaps_ref, template_ref,
                exposure_ref, slot_ref, target_ref, out_ref, grid_ref, rp_ref, windows_ref, weights_ref, ext_ref, arrived_ref, combined_ref,
                halo_send, halo_recv, grid_send, grid_recv):
    f32, bf16 = jnp.float32, jnp.bfloat16
    n_ra, n_dec = lax.axis_size("ra"), lax.axis_size("dec")
    ra, dec = lax.axis_index("ra"), lax.axis_index("dec")

    def peer(d_ra, d_dec):
        return (lax.rem(ra + d_ra + n_ra, n_ra), lax.rem(dec + d_dec + n_dec, n_dec))

    width = template_ref.shape[1]
    ext_ref[EDGE:EDGE + p_rows, TILE:TILE + width] = template_ref[...]
    partners = [(1, 0), (-1, 0), (2, 0), (-2, 0), (0, 1), (0, -1), (1, 1), (1, -1), (-1, 1), (-1, -1)]
    barrier = pltpu.get_barrier_semaphore()
    for d_ra, d_dec in partners:
        pl.semaphore_signal(barrier, inc=1, device_id=peer(d_ra, d_dec), device_id_type=MESH)

    build_weights(coef_ref, vtaps_ref, weights_ref, rp_ref, n_basis, p_rows)
    presum_rows(exposure_ref, slot_ref, target_ref, grid_ref, p_rows)
    pl.semaphore_wait(barrier, len(partners))

    top, bottom = slice(p_rows - EDGE, p_rows), slice(0, EDGE)
    left, right = slice(width - TILE, width), slice(0, TILE)
    all_rows, all_cols = slice(0, p_rows), slice(0, width)
    inner_rows, inner_cols = slice(EDGE, EDGE + p_rows), slice(TILE, TILE + width)
    low_rows, high_cols = slice(EDGE + p_rows, 2 * EDGE + p_rows), slice(TILE + width, 2 * TILE + width)
    pieces = [
        ((-1, 0), all_rows, left, inner_rows, slice(0, TILE)),
        ((1, 0), all_rows, right, inner_rows, high_cols),
        ((0, -1), top, all_cols, slice(0, EDGE), inner_cols),
        ((0, 1), bottom, all_cols, low_rows, inner_cols),
        ((-1, -1), top, left, slice(0, EDGE), slice(0, TILE)),
        ((1, -1), top, right, slice(0, EDGE), high_cols),
        ((-1, 1), bottom, left, low_rows, slice(0, TILE)),
        ((1, 1), bottom, right, low_rows, high_cols),
    ]
    halo_copies = []
    for n, ((s_ra, s_dec), my_rows, my_cols, rows, cols) in enumerate(pieces):
        copy = pltpu.make_async_remote_copy(
            src_ref=template_ref.at[my_rows, my_cols],
            dst_ref=ext_ref.at[rows, cols],
            send_sem=halo_send.at[n],
            recv_sem=halo_recv.at[n],
            device_id=peer(-s_ra, -s_dec),
            device_id_type=MESH,
        )
        copy.start()
        halo_copies.append(copy)
    sign = 2 * lax.rem(ra, 2) - 1

    def grid_copy(src, slot, d_ra):
        return pltpu.make_async_remote_copy(
            src_ref=src,
            dst_ref=arrived_ref.at[slot],
            send_sem=grid_send.at[slot],
            recv_sem=grid_recv.at[slot],
            device_id=peer(d_ra, 0),
            device_id_type=MESH,
        )

    to_partner = grid_copy(grid_ref.at[SPAN - sign], OWN, -sign)
    to_combine = grid_copy(grid_ref.at[SPAN - 2 * sign], MIXED, -sign)
    far = grid_copy(grid_ref.at[SPAN + 2 * sign], FAR, 2 * sign)
    near = grid_copy(combined_ref, NEAR, sign)
    for copy in (to_partner, to_combine, far):
        copy.start()

    to_combine.wait_recv()
    combined_ref[...] = grid_ref[SPAN + sign] + arrived_ref[MIXED]
    near.start()
    for copy in halo_copies:
        copy.wait()
    keep_top = dec > 0
    keep_bottom = dec < n_dec - 1
    ext_ref[0:EDGE, :] = jnp.where(keep_top, ext_ref[0:EDGE, :], jnp.zeros_like(ext_ref[0:EDGE, :]))
    ext_ref[EDGE + p_rows:, :] = jnp.where(
        keep_bottom, ext_ref[EDGE + p_rows:, :], jnp.zeros_like(ext_ref[EDGE + p_rows:, :])
    )
    for t in range(n_tiles):
        slab = ext_ref[:, t * TILE:t * TILE + 3 * TILE].astype(f32)
        slab = pltpu.roll(slab, 3 * TILE - (TILE - HALF), 1)
        windows_ref[t * ROWS_PAD:(t + 1) * ROWS_PAD, :] = slab[:, 0:WIN].astype(bf16)

    def row_step(step, carry):
        bands = []
        for half in range(2):
            urow = jnp.broadcast_to(utaps_ref[pl.ds(2 * step + half, 1), :], (TILE, WIN))
            bands.append(pltpu.roll(urow, 0, 1, stride=1, stride_axis=0))
        band_t = jnp.concatenate(bands, axis=0).astype(bf16)
        part = lax.dot_general(
            windows_ref[...], band_t, (((1,), (1,)), ((), ())), preferred_element_type=f32
        ).astype(bf16)
        for half in range(2):
            base = pl.multiple_of((2 * step + half) * BLOCK, BLOCK)
            for t in range(n_tiles):
                rp_ref[pl.ds(base, ROWS_PAD), t * TILE:(t + 1) * TILE] = part[
                    t * ROWS_PAD:(t + 1) * ROWS_PAD, half * TILE:(half + 1) * TILE
                ]
        return carry

    lax.fori_loop(0, n_basis // 2, row_step, 0)

    chunk = 256

    def col_step(step, carry):
        col = pl.multiple_of(step * chunk, chunk)
        sums = jnp.dot(weights_ref[...], rp_ref[:, pl.ds(col, chunk)], preferred_element_type=f32)
        lo = 3 * p_rows
        plain = sums[0:p_rows] + sums[lo:lo + p_rows]
        with_cos = sums[p_rows:2 * p_rows] + sums[lo + p_rows:lo + 2 * p_rows]
        with_sin = sums[2 * p_rows:3 * p_rows] + sums[lo + 2 * p_rows:lo + 3 * p_rows]
        cols = ra * width + col + lax.broadcasted_iota(jnp.int32, (1, chunk), 1)
        phase = (2 * cols + 1).astype(f32) * (math.pi / (width * n_ra))
        cosine = jnp.cos(phase)
        sine = jnp.sin(phase)
        out_ref[:, pl.ds(col, chunk)] = plain + cosine * with_cos + sine * with_sin
        return carry

    lax.fori_loop(0, out_ref.shape[1] // chunk, col_step, 0)

    to_partner.wait()
    to_combine.wait_send()
    far.wait()
    near.wait()
    science = grid_ref[SPAN] + arrived_ref[OWN] + arrived_ref[NEAR] + arrived_ref[FAR]
    out_ref[...] = science - out_ref[...]


def difference_image(template, exposure, slot_row, target_row, row_taps, col_taps, coef):
    p_rows, width = template.shape
    n_tiles = width // TILE
    k_count = row_taps.shape[0]
    n_basis = k_count + (k_count % 2)
    utaps = jnp.pad(row_taps.astype(jnp.float32), ((0, n_basis - k_count), (0, WIN - row_taps.shape[1])))
    vtaps = jnp.pad(col_taps.astype(jnp.float32), ((0, n_basis - k_count), (0, BLOCK - col_taps.shape[1])))
    flops = 2 * n_tiles * ROWS_PAD * WIN * n_basis * TILE + 2 * 6 * p_rows * n_basis * BLOCK * width
    vmem = pl.BlockSpec(memory_space=pltpu.VMEM)
    n_out = 2 * SPAN
    return pl.pallas_call(
        functools.partial(conv_kernel, n_tiles, n_basis, p_rows),
        out_shape=jax.ShapeDtypeStruct((p_rows, width), jnp.float32),
        in_specs=[pl.BlockSpec(memory_space=pltpu.SMEM)] + [vmem] * 6,
        out_specs=vmem,
        scratch_shapes=[
            pltpu.VMEM((2 * SPAN + 1, p_rows, width), jnp.float32),
            pltpu.VMEM((n_basis * BLOCK, width), jnp.bfloat16),
            pltpu.VMEM((n_tiles * ROWS_PAD, WIN), jnp.bfloat16),
            pltpu.VMEM((6 * p_rows, n_basis * BLOCK), jnp.bfloat16),
            pltpu.VMEM((p_rows + 2 * EDGE, width + 2 * TILE), jnp.bfloat16),
            pltpu.VMEM((n_out, p_rows, width), jnp.float32),
            pltpu.VMEM((p_rows, width), jnp.float32),
            pltpu.SemaphoreType.DMA((8,)),
            pltpu.SemaphoreType.DMA((8,)),
            pltpu.SemaphoreType.DMA((n_out,)),
            pltpu.SemaphoreType.DMA((n_out,)),
        ],
        compiler_params=pltpu.CompilerParams(
            vmem_limit_bytes=60 * 1024 * 1024, collective_id=0, has_side_effects=True
        ),
        cost_estimate=pl.CostEstimate(flops=flops, transcendentals=0, bytes_accessed=8 * 1024 * 1024),
    )(coef, utaps, vtaps, template, exposure, slot_row, target_row)


def local(exposure, slots, target_rows, template, row_taps, col_taps, coef):
    e_rows, width = exposure.shape
    p_rows = template.shape[0]
    n_slots = 2 * SPAN + 1
    slot_row = slots.reshape(1, e_rows)
    target_row = target_rows.reshape(1, e_rows)
    return difference_image(template, exposure, slot_row, target_row, row_taps, col_taps, coef)


def solution(mesh):
    return jax.shard_map(
        local,
        mesh=mesh,
        in_specs=(
            P(("ra", "dec"), None),
            P(("ra", "dec"), None),
            P(("ra", "dec")),
            P("dec", "ra"),
            P(),
            P(),
            P(),
        ),
        out_specs=P("dec", "ra"),
        check_vma=False,
    )
```

```python
import functools
import math

import jax
import jax.numpy as jnp
from jax import lax
from jax.experimental import pallas as pl
from jax.experimental.pallas import tpu as pltpu
from jax.sharding import PartitionSpec as P

SPAN = 2
HALF = 10
TILE = 128
WIN = 256
ROWS_PAD = 96
BLOCK = 128
EDGE = 16
MESH = pl.DeviceIdType.MESH
OWN, MIXED, NEAR, FAR = range(4)


def build_weights(coef_ref, vtaps_ref, weights_ref, rp_ref, n_basis, p_rows):
    f32, bf16 = jnp.float32, jnp.bfloat16
    rows = lax.axis_index("dec") * p_rows + lax.broadcasted_iota(jnp.int32, (p_rows, BLOCK), 0)
    level = (2 * rows + 1).astype(f32) / (p_rows * lax.axis_size("dec")) - 1.0
    level_sq = level * level

    def weight_step(k, carry):
        vrow = jnp.broadcast_to(vtaps_ref[pl.ds(k, 1), :], (p_rows, BLOCK))
        shifted_taps = pltpu.roll(vrow, EDGE - HALF, 1, stride=1, stride_axis=0)
        plain = coef_ref[k, 0] + coef_ref[k, 1] * level + coef_ref[k, 2] * level_sq
        with_cos = coef_ref[k, 3] + coef_ref[k, 5] * level
        col = pl.multiple_of(k * BLOCK, BLOCK)
        for term, scale in enumerate((plain, with_cos, coef_ref[k, 4])):
            w = scale * shifted_taps
            high = w.astype(bf16)
            low = (w - high.astype(f32)).astype(bf16)
            weights_ref[term * p_rows:(term + 1) * p_rows, pl.ds(col, BLOCK)] = high
            weights_ref[(3 + term) * p_rows:(4 + term) * p_rows, pl.ds(col, BLOCK)] = low
        rp_ref[pl.ds(k * BLOCK + ROWS_PAD, BLOCK - ROWS_PAD), :] = jnp.zeros(
            (BLOCK - ROWS_PAD, rp_ref.shape[1]), bf16
        )
        return carry

    k_count = coef_ref.shape[0]
    lax.fori_loop(0, k_count, weight_step, 0)
    for k in range(k_count, n_basis):
        weights_ref[:, k * BLOCK:(k + 1) * BLOCK] = jnp.zeros((weights_ref.shape[0], BLOCK), bf16)
        rp_ref[k * BLOCK + ROWS_PAD:(k + 1) * BLOCK, :] = jnp.zeros((BLOCK - ROWS_PAD, rp_ref.shape[1]), bf16)


def presum_rows(exposure_ref, slot_ref, target_ref, grid_ref, p_rows):
    f32, bf16 = jnp.float32, jnp.bfloat16
    n_slots, e_rows = grid_ref.shape[0], exposure_ref.shape[0]
    place = lax.broadcasted_iota(jnp.int32, (n_slots * p_rows, e_rows), 0)
    select = ((place // p_rows == slot_ref[...]) & (place % p_rows == target_ref[...])).astype(bf16)
    chunk = 512
    for c in range(exposure_ref.shape[1] // chunk):
        rows = exposure_ref[:, c * chunk:(c + 1) * chunk]
        first = rows.astype(bf16)
        rest = rows - first.astype(f32)
        second = rest.astype(bf16)
        third = (rest - second.astype(f32)).astype(bf16)
        total = jnp.dot(select, first, preferred_element_type=f32)
        total = total + jnp.dot(select, second, preferred_element_type=f32)
        total = total + jnp.dot(select, third, preferred_element_type=f32)
        for slot in range(n_slots):
            grid_ref[slot, :, c * chunk:(c + 1) * chunk] = total[slot * p_rows:(slot + 1) * p_rows]


def conv_kernel(n_tiles, n_basis, p_rows, coef_ref, utaps_ref, vtaps_ref, template_ref,
                exposure_ref, slot_ref, target_ref, out_ref, grid_ref, rp_ref, windows_ref, weights_ref, ext_ref, arrived_ref, combined_ref,
                halo_send, halo_recv, grid_send, grid_recv):
    f32, bf16 = jnp.float32, jnp.bfloat16
    n_ra, n_dec = lax.axis_size("ra"), lax.axis_size("dec")
    ra, dec = lax.axis_index("ra"), lax.axis_index("dec")

    def peer(d_ra, d_dec):
        return (lax.rem(ra + d_ra + n_ra, n_ra), lax.rem(dec + d_dec + n_dec, n_dec))

    width = template_ref.shape[1]
    ext_ref[EDGE:EDGE + p_rows, TILE:TILE + width] = template_ref[...]
    partners = [(1, 0), (-1, 0), (2, 0), (-2, 0), (0, 1), (0, -1), (1, 1), (1, -1), (-1, 1), (-1, -1)]
    barrier = pltpu.get_barrier_semaphore()
    for d_ra, d_dec in partners:
        pl.semaphore_signal(barrier, inc=1, device_id=peer(d_ra, d_dec), device_id_type=MESH)

    presum_rows(exposure_ref, slot_ref, target_ref, grid_ref, p_rows)
    pl.semaphore_wait(barrier, len(partners))

    top, bottom = slice(p_rows - EDGE, p_rows), slice(0, EDGE)
    left, right = slice(width - TILE, width), slice(0, TILE)
    all_rows, all_cols = slice(0, p_rows), slice(0, width)
    inner_rows, inner_cols = slice(EDGE, EDGE + p_rows), slice(TILE, TILE + width)
    low_rows, high_cols = slice(EDGE + p_rows, 2 * EDGE + p_rows), slice(TILE + width, 2 * TILE + width)
    pieces = [
        ((-1, 0), all_rows, left, inner_rows, slice(0, TILE)),
        ((1, 0), all_rows, right, inner_rows, high_cols),
        ((0, -1), top, all_cols, slice(0, EDGE), inner_cols),
        ((0, 1), bottom, all_cols, low_rows, inner_cols),
        ((-1, -1), top, left, slice(0, EDGE), slice(0, TILE)),
        ((1, -1), top, right, slice(0, EDGE), high_cols),
        ((-1, 1), bottom, left, low_rows, slice(0, TILE)),
        ((1, 1), bottom, right, low_rows, high_cols),
    ]
    halo_copies = []
    for n, ((s_ra, s_dec), my_rows, my_cols, rows, cols) in enumerate(pieces):
        copy = pltpu.make_async_remote_copy(
            src_ref=template_ref.at[my_rows, my_cols],
            dst_ref=ext_ref.at[rows, cols],
            send_sem=halo_send.at[n],
            recv_sem=halo_recv.at[n],
            device_id=peer(-s_ra, -s_dec),
            device_id_type=MESH,
        )
        copy.start()
        halo_copies.append(copy)
    sign = 2 * lax.rem(ra, 2) - 1

    def grid_copy(src, slot, d_ra):
        return pltpu.make_async_remote_copy(
            src_ref=src,
            dst_ref=arrived_ref.at[slot],
            send_sem=grid_send.at[slot],
            recv_sem=grid_recv.at[slot],
            device_id=peer(d_ra, 0),
            device_id_type=MESH,
        )

    to_partner = grid_copy(grid_ref.at[SPAN - sign], OWN, -sign)
    to_combine = grid_copy(grid_ref.at[SPAN - 2 * sign], MIXED, -sign)
    far = grid_copy(grid_ref.at[SPAN + 2 * sign], FAR, 2 * sign)
    near = grid_copy(combined_ref, NEAR, sign)
    for copy in (to_partner, to_combine, far):
        copy.start()

    to_combine.wait_recv()
    combined_ref[...] = grid_ref[SPAN + sign] + arrived_ref[MIXED]
    near.start()
    build_weights(coef_ref, vtaps_ref, weights_ref, rp_ref, n_basis, p_rows)
    for copy in halo_copies:
        copy.wait()
    keep_top = dec > 0
    keep_bottom = dec < n_dec - 1
    ext_ref[0:EDGE, :] = jnp.where(keep_top, ext_ref[0:EDGE, :], jnp.zeros_like(ext_ref[0:EDGE, :]))
    ext_ref[EDGE + p_rows:, :] = jnp.where(
        keep_bottom, ext_ref[EDGE + p_rows:, :], jnp.zeros_like(ext_ref[EDGE + p_rows:, :])
    )
    for t in range(n_tiles):
        slab = ext_ref[:, t * TILE:t * TILE + 3 * TILE].astype(f32)
        slab = pltpu.roll(slab, 3 * TILE - (TILE - HALF), 1)
        windows_ref[t * ROWS_PAD:(t + 1) * ROWS_PAD, :] = slab[:, 0:WIN].astype(bf16)

    def row_step(step, carry):
        bands = []
        for half in range(2):
            urow = jnp.broadcast_to(utaps_ref[pl.ds(2 * step + half, 1), :], (TILE, WIN))
            bands.append(pltpu.roll(urow, 0, 1, stride=1, stride_axis=0))
        band_t = jnp.concatenate(bands, axis=0).astype(bf16)
        part = lax.dot_general(
            windows_ref[...], band_t, (((1,), (1,)), ((), ())), preferred_element_type=f32
        ).astype(bf16)
        for half in range(2):
            base = pl.multiple_of((2 * step + half) * BLOCK, BLOCK)
            for t in range(n_tiles):
                rp_ref[pl.ds(base, ROWS_PAD), t * TILE:(t + 1) * TILE] = part[
                    t * ROWS_PAD:(t + 1) * ROWS_PAD, half * TILE:(half + 1) * TILE
                ]
        return carry

    lax.fori_loop(0, n_basis // 2, row_step, 0)

    chunk = 256

    def col_step(step, carry):
        col = pl.multiple_of(step * chunk, chunk)
        sums = jnp.dot(weights_ref[...], rp_ref[:, pl.ds(col, chunk)], preferred_element_type=f32)
        lo = 3 * p_rows
        plain = sums[0:p_rows] + sums[lo:lo + p_rows]
        with_cos = sums[p_rows:2 * p_rows] + sums[lo + p_rows:lo + 2 * p_rows]
        with_sin = sums[2 * p_rows:3 * p_rows] + sums[lo + 2 * p_rows:lo + 3 * p_rows]
        cols = ra * width + col + lax.broadcasted_iota(jnp.int32, (1, chunk), 1)
        phase = (2 * cols + 1).astype(f32) * (math.pi / (width * n_ra))
        cosine = jnp.cos(phase)
        sine = jnp.sin(phase)
        out_ref[:, pl.ds(col, chunk)] = plain + cosine * with_cos + sine * with_sin
        return carry

    lax.fori_loop(0, out_ref.shape[1] // chunk, col_step, 0)

    to_partner.wait()
    to_combine.wait_send()
    far.wait()
    near.wait()
    science = grid_ref[SPAN] + arrived_ref[OWN] + arrived_ref[NEAR] + arrived_ref[FAR]
    out_ref[...] = science - out_ref[...]


def difference_image(template, exposure, slot_row, target_row, row_taps, col_taps, coef):
    p_rows, width = template.shape
    n_tiles = width // TILE
    k_count = row_taps.shape[0]
    n_basis = k_count + (k_count % 2)
    utaps = jnp.pad(row_taps.astype(jnp.float32), ((0, n_basis - k_count), (0, WIN - row_taps.shape[1])))
    vtaps = jnp.pad(col_taps.astype(jnp.float32), ((0, n_basis - k_count), (0, BLOCK - col_taps.shape[1])))
    flops = 2 * n_tiles * ROWS_PAD * WIN * n_basis * TILE + 2 * 6 * p_rows * n_basis * BLOCK * width
    vmem = pl.BlockSpec(memory_space=pltpu.VMEM)
    n_out = 2 * SPAN
    return pl.pallas_call(
        functools.partial(conv_kernel, n_tiles, n_basis, p_rows),
        out_shape=jax.ShapeDtypeStruct((p_rows, width), jnp.float32),
        in_specs=[pl.BlockSpec(memory_space=pltpu.SMEM)] + [vmem] * 6,
        out_specs=vmem,
        scratch_shapes=[
            pltpu.VMEM((2 * SPAN + 1, p_rows, width), jnp.float32),
            pltpu.VMEM((n_basis * BLOCK, width), jnp.bfloat16),
            pltpu.VMEM((n_tiles * ROWS_PAD, WIN), jnp.bfloat16),
            pltpu.VMEM((6 * p_rows, n_basis * BLOCK), jnp.bfloat16),
            pltpu.VMEM((p_rows + 2 * EDGE, width + 2 * TILE), jnp.bfloat16),
            pltpu.VMEM((n_out, p_rows, width), jnp.float32),
            pltpu.VMEM((p_rows, width), jnp.float32),
            pltpu.SemaphoreType.DMA((8,)),
            pltpu.SemaphoreType.DMA((8,)),
            pltpu.SemaphoreType.DMA((n_out,)),
            pltpu.SemaphoreType.DMA((n_out,)),
        ],
        compiler_params=pltpu.CompilerParams(
            vmem_limit_bytes=60 * 1024 * 1024, collective_id=0, has_side_effects=True
        ),
        cost_estimate=pl.CostEstimate(flops=flops, transcendentals=0, bytes_accessed=8 * 1024 * 1024),
    )(coef, utaps, vtaps, template, exposure, slot_row, target_row)


def local(exposure, slots, target_rows, template, row_taps, col_taps, coef):
    e_rows, width = exposure.shape
    p_rows = template.shape[0]
    n_slots = 2 * SPAN + 1
    slot_row = slots.reshape(1, e_rows)
    target_row = target_rows.reshape(1, e_rows)
    return difference_image(template, exposure, slot_row, target_row, row_taps, col_taps, coef)


def solution(mesh):
    return jax.shard_map(
        local,
        mesh=mesh,
        in_specs=(
            P(("ra", "dec"), None),
            P(("ra", "dec"), None),
            P(("ra", "dec")),
            P("dec", "ra"),
            P(),
            P(),
            P(),
        ),
        out_specs=P("dec", "ra"),
        check_vma=False,
    )
```

```python
import functools
import math

import jax
import jax.numpy as jnp
from jax import lax
from jax.experimental import pallas as pl
from jax.experimental.pallas import tpu as pltpu
from jax.sharding import PartitionSpec as P

SPAN = 2
HALF = 10
TILE = 128
WIN = 256
ROWS_PAD = 96
BLOCK = 128
EDGE = 16
MESH = pl.DeviceIdType.MESH
OWN, MIXED, NEAR, FAR = range(4)


def build_weights(coef_ref, vtaps_ref, weights_ref, rp_ref, n_basis, p_rows):
    f32, bf16 = jnp.float32, jnp.bfloat16
    rows = lax.axis_index("dec") * p_rows + lax.broadcasted_iota(jnp.int32, (p_rows, BLOCK), 0)
    level = (2 * rows + 1).astype(f32) / (p_rows * lax.axis_size("dec")) - 1.0
    level_sq = level * level

    def weight_step(k, carry):
        vrow = jnp.broadcast_to(vtaps_ref[pl.ds(k, 1), :], (p_rows, BLOCK))
        shifted_taps = pltpu.roll(vrow, EDGE - HALF, 1, stride=1, stride_axis=0)
        plain = coef_ref[k, 0] + coef_ref[k, 1] * level + coef_ref[k, 2] * level_sq
        with_cos = coef_ref[k, 3] + coef_ref[k, 5] * level
        col = pl.multiple_of(k * BLOCK, BLOCK)
        for term, scale in enumerate((plain, with_cos, coef_ref[k, 4])):
            w = scale * shifted_taps
            high = w.astype(bf16)
            low = (w - high.astype(f32)).astype(bf16)
            weights_ref[term * p_rows:(term + 1) * p_rows, pl.ds(col, BLOCK)] = high
            weights_ref[(3 + term) * p_rows:(4 + term) * p_rows, pl.ds(col, BLOCK)] = low
        rp_ref[pl.ds(k * BLOCK + ROWS_PAD, BLOCK - ROWS_PAD), :] = jnp.zeros(
            (BLOCK - ROWS_PAD, rp_ref.shape[1]), bf16
        )
        return carry

    k_count = coef_ref.shape[0]
    lax.fori_loop(0, k_count, weight_step, 0)
    for k in range(k_count, n_basis):
        weights_ref[:, k * BLOCK:(k + 1) * BLOCK] = jnp.zeros((weights_ref.shape[0], BLOCK), bf16)
        rp_ref[k * BLOCK + ROWS_PAD:(k + 1) * BLOCK, :] = jnp.zeros((BLOCK - ROWS_PAD, rp_ref.shape[1]), bf16)


def presum_rows(exposure_ref, slot_ref, target_ref, grid_ref, p_rows):
    f32, bf16 = jnp.float32, jnp.bfloat16
    n_slots, e_rows = grid_ref.shape[0], exposure_ref.shape[0]
    place = lax.broadcasted_iota(jnp.int32, (n_slots * p_rows, e_rows), 0)
    select = ((place // p_rows == slot_ref[...]) & (place % p_rows == target_ref[...])).astype(bf16)
    chunk = 512
    for c in range(exposure_ref.shape[1] // chunk):
        rows = exposure_ref[:, c * chunk:(c + 1) * chunk]
        first = rows.astype(bf16)
        rest = rows - first.astype(f32)
        second = rest.astype(bf16)
        third = (rest - second.astype(f32)).astype(bf16)
        total = jnp.dot(select, first, preferred_element_type=f32)
        total = total + jnp.dot(select, second, preferred_element_type=f32)
        total = total + jnp.dot(select, third, preferred_element_type=f32)
        for slot in range(n_slots):
            grid_ref[slot, :, c * chunk:(c + 1) * chunk] = total[slot * p_rows:(slot + 1) * p_rows]


def conv_kernel(n_tiles, n_basis, p_rows, coef_ref, utaps_ref, vtaps_ref, template_ref,
                exposure_ref, slot_ref, target_ref, out_ref, grid_ref, rp_ref, windows_ref, weights_ref, ext_ref, arrived_ref, combined_ref,
                inner_ref, band_ref,
                halo_send, halo_recv, grid_send, grid_recv):
    f32, bf16 = jnp.float32, jnp.bfloat16
    n_ra, n_dec = lax.axis_size("ra"), lax.axis_size("dec")
    ra, dec = lax.axis_index("ra"), lax.axis_index("dec")

    def peer(d_ra, d_dec):
        return (lax.rem(ra + d_ra + n_ra, n_ra), lax.rem(dec + d_dec + n_dec, n_dec))

    width = template_ref.shape[1]
    ext_ref[EDGE:EDGE + p_rows, TILE:TILE + width] = template_ref[...]
    partners = [(1, 0), (-1, 0), (2, 0), (-2, 0), (0, 1), (0, -1), (1, 1), (1, -1), (-1, 1), (-1, -1)]
    barrier = pltpu.get_barrier_semaphore()
    for d_ra, d_dec in partners:
        pl.semaphore_signal(barrier, inc=1, device_id=peer(d_ra, d_dec), device_id_type=MESH)

    presum_rows(exposure_ref, slot_ref, target_ref, grid_ref, p_rows)
    pl.semaphore_wait(barrier, len(partners))

    top, bottom = slice(p_rows - EDGE, p_rows), slice(0, EDGE)
    left, right = slice(width - TILE, width), slice(0, TILE)
    all_rows, all_cols = slice(0, p_rows), slice(0, width)
    inner_rows, inner_cols = slice(EDGE, EDGE + p_rows), slice(TILE, TILE + width)
    low_rows, high_cols = slice(EDGE + p_rows, 2 * EDGE + p_rows), slice(TILE + width, 2 * TILE + width)
    pieces = [
        ((-1, 0), all_rows, left, inner_rows, slice(0, TILE)),
        ((1, 0), all_rows, right, inner_rows, high_cols),
        ((0, -1), top, all_cols, slice(0, EDGE), inner_cols),
        ((0, 1), bottom, all_cols, low_rows, inner_cols),
        ((-1, -1), top, left, slice(0, EDGE), slice(0, TILE)),
        ((1, -1), top, right, slice(0, EDGE), high_cols),
        ((-1, 1), bottom, left, low_rows, slice(0, TILE)),
        ((1, 1), bottom, right, low_rows, high_cols),
    ]
    halo_copies = []
    for n, ((s_ra, s_dec), my_rows, my_cols, rows, cols) in enumerate(pieces):
        copy = pltpu.make_async_remote_copy(
            src_ref=template_ref.at[my_rows, my_cols],
            dst_ref=ext_ref.at[rows, cols],
            send_sem=halo_send.at[n],
            recv_sem=halo_recv.at[n],
            device_id=peer(-s_ra, -s_dec),
            device_id_type=MESH,
        )
        copy.start()
        halo_copies.append(copy)
    sign = 2 * lax.rem(ra, 2) - 1

    def grid_copy(src, slot, d_ra):
        return pltpu.make_async_remote_copy(
            src_ref=src,
            dst_ref=arrived_ref.at[slot],
            send_sem=grid_send.at[slot],
            recv_sem=grid_recv.at[slot],
            device_id=peer(d_ra, 0),
            device_id_type=MESH,
        )

    to_partner = grid_copy(grid_ref.at[SPAN - sign], OWN, -sign)
    to_combine = grid_copy(grid_ref.at[SPAN - 2 * sign], MIXED, -sign)
    far = grid_copy(grid_ref.at[SPAN + 2 * sign], FAR, 2 * sign)
    near = grid_copy(combined_ref, NEAR, sign)
    for copy in (to_partner, to_combine, far):
        copy.start()

    to_combine.wait_recv()
    combined_ref[...] = grid_ref[SPAN + sign] + arrived_ref[MIXED]
    near.start()
    build_weights(coef_ref, vtaps_ref, weights_ref, rp_ref, n_basis, p_rows)

    inner = n_tiles - 2
    for t in range(1, n_tiles - 1):
        slab = template_ref[:, (t - 1) * TILE:(t + 2) * TILE].astype(f32)
        slab = pltpu.roll(slab, 3 * TILE - (TILE - HALF), 1)
        inner_ref[(t - 1) * p_rows:t * p_rows, :] = slab[:, 0:WIN].astype(bf16)

    def inner_step(step, carry):
        bands = []
        for half in range(2):
            urow = jnp.broadcast_to(utaps_ref[pl.ds(2 * step + half, 1), :], (TILE, WIN))
            bands.append(pltpu.roll(urow, 0, 1, stride=1, stride_axis=0))
        band_t = jnp.concatenate(bands, axis=0).astype(bf16)
        band_ref[step] = band_t
        part = lax.dot_general(
            inner_ref[...], band_t, (((1,), (1,)), ((), ())), preferred_element_type=f32
        ).astype(bf16)
        for half in range(2):
            base = pl.multiple_of((2 * step + half) * BLOCK + EDGE, EDGE)
            for t in range(1, n_tiles - 1):
                rp_ref[pl.ds(base, p_rows), t * TILE:(t + 1) * TILE] = part[
                    (t - 1) * p_rows:t * p_rows, half * TILE:(half + 1) * TILE
                ]
        return carry

    lax.fori_loop(0, n_basis // 2, inner_step, 0)

    for copy in halo_copies:
        copy.wait()
    keep_top = dec > 0
    keep_bottom = dec < n_dec - 1
    ext_ref[0:EDGE, :] = jnp.where(keep_top, ext_ref[0:EDGE, :], jnp.zeros_like(ext_ref[0:EDGE, :]))
    ext_ref[EDGE + p_rows:, :] = jnp.where(
        keep_bottom, ext_ref[EDGE + p_rows:, :], jnp.zeros_like(ext_ref[EDGE + p_rows:, :])
    )
    edge_rows = 2 * EDGE * n_tiles
    for t in range(n_tiles):
        slab = ext_ref[:, t * TILE:t * TILE + 3 * TILE].astype(f32)
        slab = pltpu.roll(slab, 3 * TILE - (TILE - HALF), 1)[:, 0:WIN].astype(bf16)
        windows_ref[2 * EDGE * t:2 * EDGE * t + EDGE, :] = slab[0:EDGE]
        windows_ref[2 * EDGE * t + EDGE:2 * EDGE * (t + 1), :] = slab[EDGE + p_rows:]
        if t in (0, n_tiles - 1):
            at = edge_rows + (0 if t == 0 else p_rows)
            windows_ref[at:at + p_rows, :] = slab[EDGE:EDGE + p_rows]

    def row_step(step, carry):
        part = lax.dot_general(
            windows_ref[...], band_ref[step], (((1,), (1,)), ((), ())), preferred_element_type=f32
        ).astype(bf16)
        for half in range(2):
            base = pl.multiple_of((2 * step + half) * BLOCK, BLOCK)
            cols = slice(half * TILE, (half + 1) * TILE)
            for t in range(n_tiles):
                tile = slice(t * TILE, (t + 1) * TILE)
                rp_ref[pl.ds(base, EDGE), tile] = part[2 * EDGE * t:2 * EDGE * t + EDGE, cols]
                rp_ref[pl.ds(base + EDGE + p_rows, EDGE), tile] = part[2 * EDGE * t + EDGE:2 * EDGE * (t + 1), cols]
            for t in (0, n_tiles - 1):
                at = edge_rows + (0 if t == 0 else p_rows)
                rp_ref[pl.ds(base + EDGE, p_rows), t * TILE:(t + 1) * TILE] = part[at:at + p_rows, cols]
        return carry

    lax.fori_loop(0, n_basis // 2, row_step, 0)

    chunk = 256

    def col_step(step, carry):
        col = pl.multiple_of(step * chunk, chunk)
        sums = jnp.dot(weights_ref[...], rp_ref[:, pl.ds(col, chunk)], preferred_element_type=f32)
        lo = 3 * p_rows
        plain = sums[0:p_rows] + sums[lo:lo + p_rows]
        with_cos = sums[p_rows:2 * p_rows] + sums[lo + p_rows:lo + 2 * p_rows]
        with_sin = sums[2 * p_rows:3 * p_rows] + sums[lo + 2 * p_rows:lo + 3 * p_rows]
        cols = ra * width + col + lax.broadcasted_iota(jnp.int32, (1, chunk), 1)
        phase = (2 * cols + 1).astype(f32) * (math.pi / (width * n_ra))
        cosine = jnp.cos(phase)
        sine = jnp.sin(phase)
        out_ref[:, pl.ds(col, chunk)] = plain + cosine * with_cos + sine * with_sin
        return carry

    lax.fori_loop(0, out_ref.shape[1] // chunk, col_step, 0)

    to_partner.wait()
    to_combine.wait_send()
    far.wait()
    near.wait()
    science = grid_ref[SPAN] + arrived_ref[OWN] + arrived_ref[NEAR] + arrived_ref[FAR]
    out_ref[...] = science - out_ref[...]


def difference_image(template, exposure, slot_row, target_row, row_taps, col_taps, coef):
    p_rows, width = template.shape
    n_tiles = width // TILE
    k_count = row_taps.shape[0]
    n_basis = k_count + (k_count % 2)
    utaps = jnp.pad(row_taps.astype(jnp.float32), ((0, n_basis - k_count), (0, WIN - row_taps.shape[1])))
    vtaps = jnp.pad(col_taps.astype(jnp.float32), ((0, n_basis - k_count), (0, BLOCK - col_taps.shape[1])))
    flops = 2 * n_tiles * ROWS_PAD * WIN * n_basis * TILE + 2 * 6 * p_rows * n_basis * BLOCK * width
    vmem = pl.BlockSpec(memory_space=pltpu.VMEM)
    n_out = 2 * SPAN
    return pl.pallas_call(
        functools.partial(conv_kernel, n_tiles, n_basis, p_rows),
        out_shape=jax.ShapeDtypeStruct((p_rows, width), jnp.float32),
        in_specs=[pl.BlockSpec(memory_space=pltpu.SMEM)] + [vmem] * 6,
        out_specs=vmem,
        scratch_shapes=[
            pltpu.VMEM((2 * SPAN + 1, p_rows, width), jnp.float32),
            pltpu.VMEM((n_basis * BLOCK, width), jnp.bfloat16),
            pltpu.VMEM((2 * EDGE * n_tiles + 2 * p_rows, WIN), jnp.bfloat16),
            pltpu.VMEM((6 * p_rows, n_basis * BLOCK), jnp.bfloat16),
            pltpu.VMEM((p_rows + 2 * EDGE, width + 2 * TILE), jnp.bfloat16),
            pltpu.VMEM((n_out, p_rows, width), jnp.float32),
            pltpu.VMEM((p_rows, width), jnp.float32),
            pltpu.VMEM(((n_tiles - 2) * p_rows, WIN), jnp.bfloat16),
            pltpu.VMEM((n_basis // 2, 2 * TILE, WIN), jnp.bfloat16),
            pltpu.SemaphoreType.DMA((8,)),
            pltpu.SemaphoreType.DMA((8,)),
            pltpu.SemaphoreType.DMA((n_out,)),
            pltpu.SemaphoreType.DMA((n_out,)),
        ],
        compiler_params=pltpu.CompilerParams(
            vmem_limit_bytes=60 * 1024 * 1024, collective_id=0, has_side_effects=True
        ),
        cost_estimate=pl.CostEstimate(flops=flops, transcendentals=0, bytes_accessed=8 * 1024 * 1024),
    )(coef, utaps, vtaps, template, exposure, slot_row, target_row)


def local(exposure, slots, target_rows, template, row_taps, col_taps, coef):
    e_rows, width = exposure.shape
    p_rows = template.shape[0]
    n_slots = 2 * SPAN + 1
    slot_row = slots.reshape(1, e_rows)
    target_row = target_rows.reshape(1, e_rows)
    return difference_image(template, exposure, slot_row, target_row, row_taps, col_taps, coef)


def solution(mesh):
    return jax.shard_map(
        local,
        mesh=mesh,
        in_specs=(
            P(("ra", "dec"), None),
            P(("ra", "dec"), None),
            P(("ra", "dec")),
            P("dec", "ra"),
            P(),
            P(),
            P(),
        ),
        out_specs=P("dec", "ra"),
        check_vma=False,
    )
```

```python
import functools
import math

import jax
import jax.numpy as jnp
from jax import lax
from jax.experimental import pallas as pl
from jax.experimental.pallas import tpu as pltpu
from jax.sharding import PartitionSpec as P

SPAN = 2
HALF = 10
TILE = 128
WIN = 256
ROWS_PAD = 96
BLOCK = 128
EDGE = 16
MESH = pl.DeviceIdType.MESH
OWN, MIXED, NEAR, FAR = range(4)


def build_weights(coef_ref, vtaps_ref, weights_ref, rp_ref, n_basis, p_rows):
    f32, bf16 = jnp.float32, jnp.bfloat16
    rows = lax.axis_index("dec") * p_rows + lax.broadcasted_iota(jnp.int32, (p_rows, BLOCK), 0)
    level = (2 * rows + 1).astype(f32) / (p_rows * lax.axis_size("dec")) - 1.0
    level_sq = level * level

    def weight_step(k, carry):
        vrow = jnp.broadcast_to(vtaps_ref[pl.ds(k, 1), :], (p_rows, BLOCK))
        shifted_taps = pltpu.roll(vrow, EDGE - HALF, 1, stride=1, stride_axis=0)
        plain = coef_ref[k, 0] + coef_ref[k, 1] * level + coef_ref[k, 2] * level_sq
        with_cos = coef_ref[k, 3] + coef_ref[k, 5] * level
        col = pl.multiple_of(k * BLOCK, BLOCK)
        for term, scale in enumerate((plain, with_cos, coef_ref[k, 4])):
            w = scale * shifted_taps
            high = w.astype(bf16)
            low = (w - high.astype(f32)).astype(bf16)
            weights_ref[term * p_rows:(term + 1) * p_rows, pl.ds(col, BLOCK)] = high
            weights_ref[(3 + term) * p_rows:(4 + term) * p_rows, pl.ds(col, BLOCK)] = low
        rp_ref[pl.ds(k * BLOCK + ROWS_PAD, BLOCK - ROWS_PAD), :] = jnp.zeros(
            (BLOCK - ROWS_PAD, rp_ref.shape[1]), bf16
        )
        return carry

    k_count = coef_ref.shape[0]
    lax.fori_loop(0, k_count, weight_step, 0)
    for k in range(k_count, n_basis):
        weights_ref[:, k * BLOCK:(k + 1) * BLOCK] = jnp.zeros((weights_ref.shape[0], BLOCK), bf16)
        rp_ref[k * BLOCK + ROWS_PAD:(k + 1) * BLOCK, :] = jnp.zeros((BLOCK - ROWS_PAD, rp_ref.shape[1]), bf16)


def presum_rows(exposure_ref, slot_ref, target_ref, grid_ref, p_rows):
    f32, bf16 = jnp.float32, jnp.bfloat16
    n_slots, e_rows = grid_ref.shape[0], exposure_ref.shape[0]
    place = lax.broadcasted_iota(jnp.int32, (n_slots * p_rows, e_rows), 0)
    select = ((place // p_rows == slot_ref[...]) & (place % p_rows == target_ref[...])).astype(bf16)
    chunk = 512
    for c in range(exposure_ref.shape[1] // chunk):
        rows = exposure_ref[:, c * chunk:(c + 1) * chunk]
        first = rows.astype(bf16)
        rest = rows - first.astype(f32)
        second = rest.astype(bf16)
        third = (rest - second.astype(f32)).astype(bf16)
        total = jnp.dot(select, first, preferred_element_type=f32)
        total = total + jnp.dot(select, second, preferred_element_type=f32)
        total = total + jnp.dot(select, third, preferred_element_type=f32)
        for slot in range(n_slots):
            grid_ref[slot, :, c * chunk:(c + 1) * chunk] = total[slot * p_rows:(slot + 1) * p_rows]


def conv_kernel(n_tiles, n_basis, p_rows, coef_ref, utaps_ref, vtaps_ref, template_ref,
                exposure_ref, slot_ref, target_ref, out_ref, grid_ref, rp_ref, windows_ref, weights_ref, ext_ref, arrived_ref, combined_ref,
                inner_ref, band_ref,
                halo_send, halo_recv, grid_send, grid_recv):
    f32, bf16 = jnp.float32, jnp.bfloat16
    n_ra, n_dec = lax.axis_size("ra"), lax.axis_size("dec")
    ra, dec = lax.axis_index("ra"), lax.axis_index("dec")

    def peer(d_ra, d_dec):
        return (lax.rem(ra + d_ra + n_ra, n_ra), lax.rem(dec + d_dec + n_dec, n_dec))

    width = template_ref.shape[1]
    ext_ref[EDGE:EDGE + p_rows, TILE:TILE + width] = template_ref[...]
    partners = [(1, 0), (-1, 0), (2, 0), (-2, 0), (0, 1), (0, -1), (1, 1), (1, -1), (-1, 1), (-1, -1)]
    barrier = pltpu.get_barrier_semaphore()
    for d_ra, d_dec in partners:
        pl.semaphore_signal(barrier, inc=1, device_id=peer(d_ra, d_dec), device_id_type=MESH)

    presum_rows(exposure_ref, slot_ref, target_ref, grid_ref, p_rows)
    pl.semaphore_wait(barrier, len(partners))

    top, bottom = slice(p_rows - EDGE, p_rows), slice(0, EDGE)
    left, right = slice(width - TILE, width), slice(0, TILE)
    all_rows, all_cols = slice(0, p_rows), slice(0, width)
    inner_rows, inner_cols = slice(EDGE, EDGE + p_rows), slice(TILE, TILE + width)
    low_rows, high_cols = slice(EDGE + p_rows, 2 * EDGE + p_rows), slice(TILE + width, 2 * TILE + width)
    pieces = [
        ((-1, 0), all_rows, left, inner_rows, slice(0, TILE)),
        ((1, 0), all_rows, right, inner_rows, high_cols),
        ((0, -1), top, all_cols, slice(0, EDGE), inner_cols),
        ((0, 1), bottom, all_cols, low_rows, inner_cols),
        ((-1, -1), top, left, slice(0, EDGE), slice(0, TILE)),
        ((1, -1), top, right, slice(0, EDGE), high_cols),
        ((-1, 1), bottom, left, low_rows, slice(0, TILE)),
        ((1, 1), bottom, right, low_rows, high_cols),
    ]
    halo_copies = []
    for n, ((s_ra, s_dec), my_rows, my_cols, rows, cols) in enumerate(pieces):
        copy = pltpu.make_async_remote_copy(
            src_ref=template_ref.at[my_rows, my_cols],
            dst_ref=ext_ref.at[rows, cols],
            send_sem=halo_send.at[n],
            recv_sem=halo_recv.at[n],
            device_id=peer(-s_ra, -s_dec),
            device_id_type=MESH,
        )
        copy.start()
        halo_copies.append(copy)
    sign = 2 * lax.rem(ra, 2) - 1

    def grid_copy(src, slot, d_ra):
        return pltpu.make_async_remote_copy(
            src_ref=src,
            dst_ref=arrived_ref.at[slot],
            send_sem=grid_send.at[slot],
            recv_sem=grid_recv.at[slot],
            device_id=peer(d_ra, 0),
            device_id_type=MESH,
        )

    to_partner = grid_copy(grid_ref.at[SPAN - sign], OWN, -sign)
    to_combine = grid_copy(grid_ref.at[SPAN - 2 * sign], MIXED, -sign)
    far = grid_copy(grid_ref.at[SPAN + 2 * sign], FAR, 2 * sign)
    near = grid_copy(combined_ref, NEAR, sign)
    for copy in (to_partner, to_combine, far):
        copy.start()

    to_combine.wait_recv()
    combined_ref[...] = grid_ref[SPAN + sign] + arrived_ref[MIXED]
    near.start()
    build_weights(coef_ref, vtaps_ref, weights_ref, rp_ref, n_basis, p_rows)

    inner = n_tiles - 2
    for t in range(1, n_tiles - 1):
        slab = template_ref[:, (t - 1) * TILE:(t + 2) * TILE].astype(f32)
        slab = pltpu.roll(slab, 3 * TILE - (TILE - HALF), 1)
        inner_ref[(t - 1) * p_rows:t * p_rows, :] = slab[:, 0:WIN].astype(bf16)

    def inner_step(step, carry):
        bands = []
        for half in range(2):
            urow = jnp.broadcast_to(utaps_ref[pl.ds(2 * step + half, 1), :], (TILE, WIN))
            bands.append(pltpu.roll(urow, 0, 1, stride=1, stride_axis=0))
        band_t = jnp.concatenate(bands, axis=0).astype(bf16)
        band_ref[step] = band_t
        part = lax.dot_general(
            inner_ref[...], band_t, (((1,), (1,)), ((), ())), preferred_element_type=f32
        ).astype(bf16)
        for half in range(2):
            base = pl.multiple_of((2 * step + half) * BLOCK + EDGE, EDGE)
            for t in range(1, n_tiles - 1):
                rp_ref[pl.ds(base, p_rows), t * TILE:(t + 1) * TILE] = part[
                    (t - 1) * p_rows:t * p_rows, half * TILE:(half + 1) * TILE
                ]
        return carry

    lax.fori_loop(0, n_basis // 2, inner_step, 0)

    for copy in halo_copies:
        copy.wait()
    keep_top = dec > 0
    keep_bottom = dec < n_dec - 1
    ext_ref[0:EDGE, :] = jnp.where(keep_top, ext_ref[0:EDGE, :], jnp.zeros_like(ext_ref[0:EDGE, :]))
    ext_ref[EDGE + p_rows:, :] = jnp.where(
        keep_bottom, ext_ref[EDGE + p_rows:, :], jnp.zeros_like(ext_ref[EDGE + p_rows:, :])
    )
    edge_rows = 2 * EDGE * n_tiles
    shift = 3 * TILE - (TILE - HALF)
    for t in range(n_tiles):
        cols = slice(t * TILE, t * TILE + 3 * TILE)
        for rows, at in ((slice(0, EDGE), 2 * EDGE * t), (slice(EDGE + p_rows, 2 * EDGE + p_rows), 2 * EDGE * t + EDGE)):
            slab = pltpu.roll(ext_ref[rows, cols].astype(f32), shift, 1)
            windows_ref[at:at + EDGE, :] = slab[:, 0:WIN].astype(bf16)
        if t in (0, n_tiles - 1):
            at = edge_rows + (0 if t == 0 else p_rows)
            slab = pltpu.roll(ext_ref[EDGE:EDGE + p_rows, cols].astype(f32), shift, 1)
            windows_ref[at:at + p_rows, :] = slab[:, 0:WIN].astype(bf16)

    def row_step(step, carry):
        part = lax.dot_general(
            windows_ref[...], band_ref[step], (((1,), (1,)), ((), ())), preferred_element_type=f32
        ).astype(bf16)
        for half in range(2):
            base = pl.multiple_of((2 * step + half) * BLOCK, BLOCK)
            cols = slice(half * TILE, (half + 1) * TILE)
            for t in range(n_tiles):
                tile = slice(t * TILE, (t + 1) * TILE)
                rp_ref[pl.ds(base, EDGE), tile] = part[2 * EDGE * t:2 * EDGE * t + EDGE, cols]
                rp_ref[pl.ds(base + EDGE + p_rows, EDGE), tile] = part[2 * EDGE * t + EDGE:2 * EDGE * (t + 1), cols]
            for t in (0, n_tiles - 1):
                at = edge_rows + (0 if t == 0 else p_rows)
                rp_ref[pl.ds(base + EDGE, p_rows), t * TILE:(t + 1) * TILE] = part[at:at + p_rows, cols]
        return carry

    lax.fori_loop(0, n_basis // 2, row_step, 0)

    chunk = 256

    def col_step(step, carry):
        col = pl.multiple_of(step * chunk, chunk)
        sums = jnp.dot(weights_ref[...], rp_ref[:, pl.ds(col, chunk)], preferred_element_type=f32)
        lo = 3 * p_rows
        plain = sums[0:p_rows] + sums[lo:lo + p_rows]
        with_cos = sums[p_rows:2 * p_rows] + sums[lo + p_rows:lo + 2 * p_rows]
        with_sin = sums[2 * p_rows:3 * p_rows] + sums[lo + 2 * p_rows:lo + 3 * p_rows]
        cols = ra * width + col + lax.broadcasted_iota(jnp.int32, (1, chunk), 1)
        phase = (2 * cols + 1).astype(f32) * (math.pi / (width * n_ra))
        cosine = jnp.cos(phase)
        sine = jnp.sin(phase)
        out_ref[:, pl.ds(col, chunk)] = plain + cosine * with_cos + sine * with_sin
        return carry

    lax.fori_loop(0, out_ref.shape[1] // chunk, col_step, 0)

    to_partner.wait()
    to_combine.wait_send()
    far.wait()
    near.wait()
    science = grid_ref[SPAN] + arrived_ref[OWN] + arrived_ref[NEAR] + arrived_ref[FAR]
    out_ref[...] = science - out_ref[...]


def difference_image(template, exposure, slot_row, target_row, row_taps, col_taps, coef):
    p_rows, width = template.shape
    n_tiles = width // TILE
    k_count = row_taps.shape[0]
    n_basis = k_count + (k_count % 2)
    utaps = jnp.pad(row_taps.astype(jnp.float32), ((0, n_basis - k_count), (0, WIN - row_taps.shape[1])))
    vtaps = jnp.pad(col_taps.astype(jnp.float32), ((0, n_basis - k_count), (0, BLOCK - col_taps.shape[1])))
    flops = 2 * n_tiles * ROWS_PAD * WIN * n_basis * TILE + 2 * 6 * p_rows * n_basis * BLOCK * width
    vmem = pl.BlockSpec(memory_space=pltpu.VMEM)
    n_out = 2 * SPAN
    return pl.pallas_call(
        functools.partial(conv_kernel, n_tiles, n_basis, p_rows),
        out_shape=jax.ShapeDtypeStruct((p_rows, width), jnp.float32),
        in_specs=[pl.BlockSpec(memory_space=pltpu.SMEM)] + [vmem] * 6,
        out_specs=vmem,
        scratch_shapes=[
            pltpu.VMEM((2 * SPAN + 1, p_rows, width), jnp.float32),
            pltpu.VMEM((n_basis * BLOCK, width), jnp.bfloat16),
            pltpu.VMEM((2 * EDGE * n_tiles + 2 * p_rows, WIN), jnp.bfloat16),
            pltpu.VMEM((6 * p_rows, n_basis * BLOCK), jnp.bfloat16),
            pltpu.VMEM((p_rows + 2 * EDGE, width + 2 * TILE), jnp.bfloat16),
            pltpu.VMEM((n_out, p_rows, width), jnp.float32),
            pltpu.VMEM((p_rows, width), jnp.float32),
            pltpu.VMEM(((n_tiles - 2) * p_rows, WIN), jnp.bfloat16),
            pltpu.VMEM((n_basis // 2, 2 * TILE, WIN), jnp.bfloat16),
            pltpu.SemaphoreType.DMA((8,)),
            pltpu.SemaphoreType.DMA((8,)),
            pltpu.SemaphoreType.DMA((n_out,)),
            pltpu.SemaphoreType.DMA((n_out,)),
        ],
        compiler_params=pltpu.CompilerParams(
            vmem_limit_bytes=60 * 1024 * 1024, collective_id=0, has_side_effects=True
        ),
        cost_estimate=pl.CostEstimate(flops=flops, transcendentals=0, bytes_accessed=8 * 1024 * 1024),
    )(coef, utaps, vtaps, template, exposure, slot_row, target_row)


def local(exposure, slots, target_rows, template, row_taps, col_taps, coef):
    e_rows, width = exposure.shape
    p_rows = template.shape[0]
    n_slots = 2 * SPAN + 1
    slot_row = slots.reshape(1, e_rows)
    target_row = target_rows.reshape(1, e_rows)
    return difference_image(template, exposure, slot_row, target_row, row_taps, col_taps, coef)


def solution(mesh):
    return jax.shard_map(
        local,
        mesh=mesh,
        in_specs=(
            P(("ra", "dec"), None),
            P(("ra", "dec"), None),
            P(("ra", "dec")),
            P("dec", "ra"),
            P(),
            P(),
            P(),
        ),
        out_specs=P("dec", "ra"),
        check_vma=False,
    )
```

```python
import functools
import math

import jax
import jax.numpy as jnp
from jax import lax
from jax.experimental import pallas as pl
from jax.experimental.pallas import tpu as pltpu
from jax.sharding import PartitionSpec as P

SPAN = 2
HALF = 10
TILE = 128
WIN = 256
ROWS_PAD = 96
BLOCK = 128
EDGE = 16
MESH = pl.DeviceIdType.MESH
OWN, MIXED, NEAR, FAR = range(4)


def build_weights(coef_ref, vtaps_ref, weights_ref, rp_ref, n_basis, p_rows):
    f32, bf16 = jnp.float32, jnp.bfloat16
    rows = lax.axis_index("dec") * p_rows + lax.broadcasted_iota(jnp.int32, (p_rows, BLOCK), 0)
    level = (2 * rows + 1).astype(f32) / (p_rows * lax.axis_size("dec")) - 1.0
    level_sq = level * level

    def weight_step(k, carry):
        vrow = jnp.broadcast_to(vtaps_ref[pl.ds(k, 1), :], (p_rows, BLOCK))
        shifted_taps = pltpu.roll(vrow, EDGE - HALF, 1, stride=1, stride_axis=0)
        plain = coef_ref[k, 0] + coef_ref[k, 1] * level + coef_ref[k, 2] * level_sq
        with_cos = coef_ref[k, 3] + coef_ref[k, 5] * level
        col = pl.multiple_of(k * BLOCK, BLOCK)
        for term, scale in enumerate((plain, with_cos, coef_ref[k, 4])):
            w = scale * shifted_taps
            high = w.astype(bf16)
            low = (w - high.astype(f32)).astype(bf16)
            weights_ref[term * p_rows:(term + 1) * p_rows, pl.ds(col, BLOCK)] = high
            weights_ref[(3 + term) * p_rows:(4 + term) * p_rows, pl.ds(col, BLOCK)] = low
        rp_ref[pl.ds(k * BLOCK + ROWS_PAD, BLOCK - ROWS_PAD), :] = jnp.zeros(
            (BLOCK - ROWS_PAD, rp_ref.shape[1]), bf16
        )
        return carry

    k_count = coef_ref.shape[0]
    lax.fori_loop(0, k_count, weight_step, 0)
    for k in range(k_count, n_basis):
        weights_ref[:, k * BLOCK:(k + 1) * BLOCK] = jnp.zeros((weights_ref.shape[0], BLOCK), bf16)
        rp_ref[k * BLOCK + ROWS_PAD:(k + 1) * BLOCK, :] = jnp.zeros((BLOCK - ROWS_PAD, rp_ref.shape[1]), bf16)


def presum_rows(exposure_ref, slot_ref, target_ref, grid_ref, p_rows):
    f32, bf16 = jnp.float32, jnp.bfloat16
    n_slots, e_rows = grid_ref.shape[0], exposure_ref.shape[0]
    place = lax.broadcasted_iota(jnp.int32, (n_slots * p_rows, e_rows), 0)
    select = ((place // p_rows == slot_ref[...]) & (place % p_rows == target_ref[...])).astype(bf16)
    chunk = 512
    for c in range(exposure_ref.shape[1] // chunk):
        rows = exposure_ref[:, c * chunk:(c + 1) * chunk]
        first = rows.astype(bf16)
        rest = rows - first.astype(f32)
        second = rest.astype(bf16)
        third = (rest - second.astype(f32)).astype(bf16)
        total = jnp.dot(select, first, preferred_element_type=f32)
        total = total + jnp.dot(select, second, preferred_element_type=f32)
        total = total + jnp.dot(select, third, preferred_element_type=f32)
        for slot in range(n_slots):
            grid_ref[slot, :, c * chunk:(c + 1) * chunk] = total[slot * p_rows:(slot + 1) * p_rows]


def conv_kernel(n_tiles, n_basis, p_rows, coef_ref, utaps_ref, vtaps_ref, template_ref,
                exposure_ref, slot_ref, target_ref, out_ref, grid_ref, rp_ref, windows_ref, weights_ref, ext_ref, arrived_ref, combined_ref,
                inner_ref, band_ref,
                halo_send, halo_recv, grid_send, grid_recv):
    f32, bf16 = jnp.float32, jnp.bfloat16
    n_ra, n_dec = lax.axis_size("ra"), lax.axis_size("dec")
    ra, dec = lax.axis_index("ra"), lax.axis_index("dec")

    def peer(d_ra, d_dec):
        return (lax.rem(ra + d_ra + n_ra, n_ra), lax.rem(dec + d_dec + n_dec, n_dec))

    width = template_ref.shape[1]
    ext_ref[EDGE:EDGE + p_rows, TILE:TILE + width] = template_ref[...]
    partners = [(1, 0), (-1, 0), (2, 0), (-2, 0), (0, 1), (0, -1), (1, 1), (1, -1), (-1, 1), (-1, -1)]
    barrier = pltpu.get_barrier_semaphore()
    for d_ra, d_dec in partners:
        pl.semaphore_signal(barrier, inc=1, device_id=peer(d_ra, d_dec), device_id_type=MESH)

    presum_rows(exposure_ref, slot_ref, target_ref, grid_ref, p_rows)
    pl.semaphore_wait(barrier, len(partners))

    top, bottom = slice(p_rows - EDGE, p_rows), slice(0, EDGE)
    left, right = slice(width - TILE, width), slice(0, TILE)
    all_rows, all_cols = slice(0, p_rows), slice(0, width)
    inner_rows, inner_cols = slice(EDGE, EDGE + p_rows), slice(TILE, TILE + width)
    low_rows, high_cols = slice(EDGE + p_rows, 2 * EDGE + p_rows), slice(TILE + width, 2 * TILE + width)
    pieces = [
        ((-1, 0), all_rows, left, inner_rows, slice(0, TILE)),
        ((1, 0), all_rows, right, inner_rows, high_cols),
        ((0, -1), top, all_cols, slice(0, EDGE), inner_cols),
        ((0, 1), bottom, all_cols, low_rows, inner_cols),
        ((-1, -1), top, left, slice(0, EDGE), slice(0, TILE)),
        ((1, -1), top, right, slice(0, EDGE), high_cols),
        ((-1, 1), bottom, left, low_rows, slice(0, TILE)),
        ((1, 1), bottom, right, low_rows, high_cols),
    ]
    halo_copies = []
    for n, ((s_ra, s_dec), my_rows, my_cols, rows, cols) in enumerate(pieces):
        copy = pltpu.make_async_remote_copy(
            src_ref=template_ref.at[my_rows, my_cols],
            dst_ref=ext_ref.at[rows, cols],
            send_sem=halo_send.at[n],
            recv_sem=halo_recv.at[n],
            device_id=peer(-s_ra, -s_dec),
            device_id_type=MESH,
        )
        copy.start()
        halo_copies.append(copy)
    sign = 2 * lax.rem(ra, 2) - 1

    def grid_copy(src, slot, d_ra):
        return pltpu.make_async_remote_copy(
            src_ref=src,
            dst_ref=arrived_ref.at[slot],
            send_sem=grid_send.at[slot],
            recv_sem=grid_recv.at[slot],
            device_id=peer(d_ra, 0),
            device_id_type=MESH,
        )

    to_partner = grid_copy(grid_ref.at[SPAN - sign], OWN, -sign)
    to_combine = grid_copy(grid_ref.at[SPAN - 2 * sign], MIXED, -sign)
    far = grid_copy(grid_ref.at[SPAN + 2 * sign], FAR, 2 * sign)
    near = grid_copy(combined_ref, NEAR, sign)
    for copy in (to_partner, to_combine, far):
        copy.start()

    to_combine.wait_recv()
    combined_ref[...] = grid_ref[SPAN + sign] + arrived_ref[MIXED]
    near.start()
    build_weights(coef_ref, vtaps_ref, weights_ref, rp_ref, n_basis, p_rows)

    inner = n_tiles - 2
    for t in range(1, n_tiles - 1):
        slab = template_ref[:, (t - 1) * TILE:(t + 2) * TILE].astype(f32)
        slab = pltpu.roll(slab, 3 * TILE - (TILE - HALF), 1)
        inner_ref[(t - 1) * p_rows:t * p_rows, :] = slab[:, 0:WIN].astype(bf16)

    def inner_step(step, carry):
        bands = []
        for half in range(2):
            urow = jnp.broadcast_to(utaps_ref[pl.ds(2 * step + half, 1), :], (TILE, WIN))
            bands.append(pltpu.roll(urow, 0, 1, stride=1, stride_axis=0))
        band_t = jnp.concatenate(bands, axis=0).astype(bf16)
        band_ref[step] = band_t
        part = lax.dot_general(
            inner_ref[...], band_t, (((1,), (1,)), ((), ())), preferred_element_type=f32
        ).astype(bf16)
        for half in range(2):
            base = pl.multiple_of((2 * step + half) * BLOCK + EDGE, EDGE)
            for t in range(1, n_tiles - 1):
                rp_ref[pl.ds(base, p_rows), t * TILE:(t + 1) * TILE] = part[
                    (t - 1) * p_rows:t * p_rows, half * TILE:(half + 1) * TILE
                ]
        return carry

    lax.fori_loop(0, n_basis // 2, inner_step, 0)

    for copy in halo_copies:
        copy.wait()
    keep_top = dec > 0
    keep_bottom = dec < n_dec - 1
    ext_ref[0:EDGE, :] = jnp.where(keep_top, ext_ref[0:EDGE, :], jnp.zeros_like(ext_ref[0:EDGE, :]))
    ext_ref[EDGE + p_rows:, :] = jnp.where(
        keep_bottom, ext_ref[EDGE + p_rows:, :], jnp.zeros_like(ext_ref[EDGE + p_rows:, :])
    )
    edge_rows = 2 * EDGE * n_tiles
    shift = 3 * TILE - (TILE - HALF)
    for t in range(n_tiles):
        cols = slice(t * TILE, t * TILE + 3 * TILE)
        for rows, at in ((slice(0, EDGE), 2 * EDGE * t), (slice(EDGE + p_rows, 2 * EDGE + p_rows), 2 * EDGE * t + EDGE)):
            slab = pltpu.roll(ext_ref[rows, cols].astype(f32), shift, 1)
            windows_ref[at:at + EDGE, :] = slab[:, 0:WIN].astype(bf16)
        if t in (0, n_tiles - 1):
            at = edge_rows + (0 if t == 0 else p_rows)
            slab = pltpu.roll(ext_ref[EDGE:EDGE + p_rows, cols].astype(f32), shift, 1)
            windows_ref[at:at + p_rows, :] = slab[:, 0:WIN].astype(bf16)

    def row_step(step, carry):
        part = lax.dot_general(
            windows_ref[...], band_ref[step], (((1,), (1,)), ((), ())), preferred_element_type=f32
        ).astype(bf16)
        for half in range(2):
            base = pl.multiple_of((2 * step + half) * BLOCK, BLOCK)
            cols = slice(half * TILE, (half + 1) * TILE)
            for t in range(n_tiles):
                tile = slice(t * TILE, (t + 1) * TILE)
                rp_ref[pl.ds(base, EDGE), tile] = part[2 * EDGE * t:2 * EDGE * t + EDGE, cols]
                rp_ref[pl.ds(base + EDGE + p_rows, EDGE), tile] = part[2 * EDGE * t + EDGE:2 * EDGE * (t + 1), cols]
            for t in (0, n_tiles - 1):
                at = edge_rows + (0 if t == 0 else p_rows)
                rp_ref[pl.ds(base + EDGE, p_rows), t * TILE:(t + 1) * TILE] = part[at:at + p_rows, cols]
        return carry

    lax.fori_loop(0, n_basis // 2, row_step, 0)

    chunk = 512

    def col_step(step, carry):
        col = pl.multiple_of(step * chunk, chunk)
        sums = jnp.dot(weights_ref[...], rp_ref[:, pl.ds(col, chunk)], preferred_element_type=f32)
        lo = 3 * p_rows
        plain = sums[0:p_rows] + sums[lo:lo + p_rows]
        with_cos = sums[p_rows:2 * p_rows] + sums[lo + p_rows:lo + 2 * p_rows]
        with_sin = sums[2 * p_rows:3 * p_rows] + sums[lo + 2 * p_rows:lo + 3 * p_rows]
        cols = ra * width + col + lax.broadcasted_iota(jnp.int32, (1, chunk), 1)
        phase = (2 * cols + 1).astype(f32) * (math.pi / (width * n_ra))
        cosine = jnp.cos(phase)
        sine = jnp.sin(phase)
        out_ref[:, pl.ds(col, chunk)] = plain + cosine * with_cos + sine * with_sin
        return carry

    lax.fori_loop(0, out_ref.shape[1] // chunk, col_step, 0)

    to_partner.wait()
    to_combine.wait_send()
    far.wait()
    near.wait()
    science = grid_ref[SPAN] + arrived_ref[OWN] + arrived_ref[NEAR] + arrived_ref[FAR]
    out_ref[...] = science - out_ref[...]


def difference_image(template, exposure, slot_row, target_row, row_taps, col_taps, coef):
    p_rows, width = template.shape
    n_tiles = width // TILE
    k_count = row_taps.shape[0]
    n_basis = k_count + (k_count % 2)
    utaps = jnp.pad(row_taps.astype(jnp.float32), ((0, n_basis - k_count), (0, WIN - row_taps.shape[1])))
    vtaps = jnp.pad(col_taps.astype(jnp.float32), ((0, n_basis - k_count), (0, BLOCK - col_taps.shape[1])))
    flops = 2 * n_tiles * ROWS_PAD * WIN * n_basis * TILE + 2 * 6 * p_rows * n_basis * BLOCK * width
    vmem = pl.BlockSpec(memory_space=pltpu.VMEM)
    n_out = 2 * SPAN
    return pl.pallas_call(
        functools.partial(conv_kernel, n_tiles, n_basis, p_rows),
        out_shape=jax.ShapeDtypeStruct((p_rows, width), jnp.float32),
        in_specs=[pl.BlockSpec(memory_space=pltpu.SMEM)] + [vmem] * 6,
        out_specs=vmem,
        scratch_shapes=[
            pltpu.VMEM((2 * SPAN + 1, p_rows, width), jnp.float32),
            pltpu.VMEM((n_basis * BLOCK, width), jnp.bfloat16),
            pltpu.VMEM((2 * EDGE * n_tiles + 2 * p_rows, WIN), jnp.bfloat16),
            pltpu.VMEM((6 * p_rows, n_basis * BLOCK), jnp.bfloat16),
            pltpu.VMEM((p_rows + 2 * EDGE, width + 2 * TILE), jnp.bfloat16),
            pltpu.VMEM((n_out, p_rows, width), jnp.float32),
            pltpu.VMEM((p_rows, width), jnp.float32),
            pltpu.VMEM(((n_tiles - 2) * p_rows, WIN), jnp.bfloat16),
            pltpu.VMEM((n_basis // 2, 2 * TILE, WIN), jnp.bfloat16),
            pltpu.SemaphoreType.DMA((8,)),
            pltpu.SemaphoreType.DMA((8,)),
            pltpu.SemaphoreType.DMA((n_out,)),
            pltpu.SemaphoreType.DMA((n_out,)),
        ],
        compiler_params=pltpu.CompilerParams(
            vmem_limit_bytes=60 * 1024 * 1024, collective_id=0, has_side_effects=True
        ),
        cost_estimate=pl.CostEstimate(flops=flops, transcendentals=0, bytes_accessed=8 * 1024 * 1024),
    )(coef, utaps, vtaps, template, exposure, slot_row, target_row)


def local(exposure, slots, target_rows, template, row_taps, col_taps, coef):
    e_rows, width = exposure.shape
    p_rows = template.shape[0]
    n_slots = 2 * SPAN + 1
    slot_row = slots.reshape(1, e_rows)
    target_row = target_rows.reshape(1, e_rows)
    return difference_image(template, exposure, slot_row, target_row, row_taps, col_taps, coef)


def solution(mesh):
    return jax.shard_map(
        local,
        mesh=mesh,
        in_specs=(
            P(("ra", "dec"), None),
            P(("ra", "dec"), None),
            P(("ra", "dec")),
            P("dec", "ra"),
            P(),
            P(),
            P(),
        ),
        out_specs=P("dec", "ra"),
        check_vma=False,
    )
```
